32 devices in a mesh: row: 4 (over z), col: 8 (over y, x, core).
Axes of the slice: x: 2, y: 2, z: 4, core: 2. Of those that a mesh axis runs over, the one named last changes fastest.
Arguments:
- points: float32 [16, 1024], P(None, ('row', 'col')), may hold values from -6 to 6
- pivots_first: int32 [128], replicated, may hold values from 0 to 1023, as said below
- pivots_second: int32 [128], replicated, may hold values from 0 to 1023, as said below
Outputs:
- panels: float32 [1024, 256], P('row')
- schur: float32 [1024, 1024], P('row', 'col')
The draws below stay inside these ranges and needn't reach their ends.
Inputs may be any that keep to these rules, and one draw needn't show every extreme that they name: `pivots_first`: 128 distinct indices, none of them among pivots_second. `pivots_second`: 128 distinct indices, none of them among pivots_first.
All inputs are finite; a program needn't handle non-finite values.
Results may differ from the reference program's by a relative error of at most 0.0003.
Values sent between devices are 32-bit elements; how exact they have to be, the bound alone decides.
No kernel may reach another device: no remote copies, remote signals or barrier semaphores. Data moves between devices by JAX's collectives and lax.ppermute only.
A program may use at most 64 MiB of HBM per device.

```python
import jax
import jax.numpy as jnp
from jax import lax

DIM = 16
BLOCK = 128
NPTS = 1024
N_ROW = 4


def pivot_order(key):
    return jax.random.permutation(jax.random.fold_in(key, 11), NPTS)[:2 * BLOCK].astype(jnp.int32)


def draw_pivots_first(key, part):
    return pivot_order(key)[:BLOCK]


def draw_pivots_second(key, part):
    return pivot_order(key)[BLOCK:]


def steps_of(key, shape, pieces, smallest, high):
    def one(dim, shards_of):
        steps = jax.random.uniform(jax.random.fold_in(jax.random.fold_in(key, 6), dim), (shards_of,), jnp.float32, smallest / len(pieces), high / len(pieces))
        return jnp.repeat(jnp.exp(steps), shape[dim] // shards_of).reshape((-1,) + (1,) * (len(shape) - dim - 1))

    factor_of = one(*pieces[0])
    for cut in pieces[1:]:
        factor_of = factor_of * one(*cut)
    return factor_of


def scatter_about(key, shape, spread, bound, split=(), held_as=jnp.bfloat16):
    entries = spread * jax.random.normal(key, shape, jnp.float32)
    if split:
        entries = entries * steps_of(key, shape, split, -0.22, 0.18)
    return jnp.clip(entries, -bound, bound).astype(held_as)


def setup_inputs(seed: int = 0) -> dict:
    streams_of = jax.random.split(jax.random.key(seed), 4)
    return {
        "points": scatter_about(streams_of[0], (DIM, NPTS), 1.0, 6.0, ((1, 32),), jnp.float32),
        "pivots_first": draw_pivots_first(jax.random.fold_in(streams_of[3], 71), 0),
        "pivots_second": draw_pivots_second(jax.random.fold_in(streams_of[3], 71), 0),
    }


def kernel(left, left_ids, right, right_ids):
    left_sq = jnp.sum(left * left, axis=0)
    right_sq = jnp.sum(right * right, axis=0)
    inner = jnp.dot(left.T, right, precision=lax.Precision.HIGHEST)
    dist = left_sq[:, None] + right_sq[None, :] - 2.0 * inner
    same = (left_ids[:, None] == right_ids[None, :]).astype(jnp.float32)
    return jnp.exp(-dist / DIM) + 0.1 * same

def right_solve(root, columns):
    return jax.scipy.linalg.solve_triangular(root, columns.T, lower=True).T

def reference(points, pivots_first, pivots_second):
    ids = jnp.arange(NPTS, dtype=jnp.int32)
    first_pts = points[:, pivots_first]
    second_pts = points[:, pivots_second]
    first_columns = kernel(points, ids, first_pts, pivots_first)
    first_root = jnp.linalg.cholesky(first_columns[pivots_first])
    first_panel = right_solve(first_root, first_columns)
    first_pivot_rows = first_panel[pivots_second]
    second_columns = kernel(points, ids, second_pts, pivots_second) - jnp.dot(first_panel, first_pivot_rows.T, precision=lax.Precision.HIGHEST)
    second_root = jnp.linalg.cholesky(second_columns[pivots_second])
    second_panel = right_solve(second_root, second_columns)
    panels = jnp.concatenate([first_panel, second_panel], axis=1)
    rows_blk = NPTS // N_ROW
    blocks_pts = points.reshape(DIM, N_ROW, rows_blk).transpose(1, 0, 2)
    blocks_ids = ids.reshape(N_ROW, rows_blk)
    blocks_pan = panels.reshape(N_ROW, rows_blk, 2 * BLOCK)

    def one_block(item):
        blk_pts, blk_ids, blk_pan = item
        whole = kernel(blk_pts, blk_ids, points, ids)
        return whole - jnp.dot(blk_pan, panels.T, precision=lax.Precision.HIGHEST)
    schur = lax.map(one_block, (blocks_pts, blocks_ids, blocks_pan)).reshape(NPTS, NPTS)
    return (panels, schur)
```

```python
import functools

import jax
import jax.numpy as jnp
from jax import lax
from jax.experimental import pallas as pl
from jax.experimental.pallas import tpu as pltpu
from jax.sharding import PartitionSpec as P

DIM = 16
LANES = 128
SUB = 8
HALF = 16
PANEL = 32
PER_ROW = LANES // DIM
F32 = jnp.float32
BF16 = jnp.bfloat16
NN = (((1,), (0,)), ((), ()))
NT = (((1,), (1,)), ((), ()))
TN = (((0,), (0,)), ((), ()))


def dot(a, b, dims):
    return lax.dot_general(a, b, dims, preferred_element_type=F32)


def split2(a):
    hi = a.astype(BF16)
    return hi, (a - hi.astype(F32)).astype(BF16)


def split3(a):
    hi = a.astype(BF16)
    rest = a - hi.astype(F32)
    mid = rest.astype(BF16)
    return hi, mid, (rest - mid.astype(F32)).astype(BF16)


def dot_f32(a, b, dims):
    a_hi, a_lo = split2(a)
    b_hi, b_lo = split2(b)
    return dot(a_hi, b_hi, dims) + (dot(a_hi, b_lo, dims) + dot(a_lo, b_hi, dims))


def dot6(a, b, dims):
    a0, a1, a2 = split3(a)
    b0, b1, b2 = split3(b)
    return dot(a0, b0, dims) + ((dot(a0, b1, dims) + dot(a1, b0, dims)) + (dot(a1, b1, dims) + (dot(a0, b2, dims) + dot(a2, b0, dims))))

def exp_dist(left, right):
    left_sq = jnp.sum(left * left, axis=1, keepdims=True)
    ones = jnp.ones((SUB, DIM), F32)
    right_sq = lax.dot_general(ones, right * right, NT, precision=lax.Precision.HIGHEST, preferred_element_type=F32)[:1]
    inner = lax.dot_general(left, right, NT, precision=lax.Precision.HIGHEST, preferred_element_type=F32)
    return jnp.exp((left_sq + right_sq - 2.0 * inner) * (-1.0 / DIM))


def unpack_points(table, select, segment):
    n = segment.shape[0]
    lane = lax.broadcasted_iota(jnp.int32, (n, LANES), 1)
    keep = (lane // DIM) == segment
    fold = (lax.broadcasted_iota(jnp.int32, (LANES, DIM), 0) % DIM == lax.broadcasted_iota(jnp.int32, (LANES, DIM), 1)).astype(BF16)
    total = None
    for part in split3(table):
        row = dot(select, part, NN)
        x = dot(jnp.where(keep, row, 0.0).astype(BF16), fold, NN)
        total = x if total is None else total + x
    return total


def run_points(table_ref, start, count):
    rows = count // PER_ROW
    table = table_ref[pl.ds(pl.multiple_of(start // PER_ROW, SUB), rows), :]
    ids = lax.broadcasted_iota(jnp.int32, (count, rows), 0)
    select = (ids // PER_ROW == lax.broadcasted_iota(jnp.int32, (count, rows), 1)).astype(BF16)
    segment = lax.broadcasted_iota(jnp.int32, (count, 1), 0) % PER_ROW
    return unpack_points(table, select, segment)


def row_of(tile, s):
    return jnp.broadcast_to(tile[s : s + 1, :], (SUB, LANES))


def eliminate(rows, first_lane, n_tiles):
    sub = lax.broadcasted_iota(jnp.int32, (SUB, LANES), 0)
    lane = lax.broadcasted_iota(jnp.int32, (SUB, LANES), 1)
    at, off = first_lane // LANES, first_lane % LANES
    n_lt = len(rows[0])
    cols = [
        [jnp.broadcast_to(rows[i][at][:, off + j : off + j + 1], (SUB, LANES)) if i >= j // SUB else None for i in range(n_tiles)]
        for j in range(HALF)
    ]
    own = (lane >= off) & (lane < off + HALF)
    for i in range(n_tiles):
        unit = (lane == off + i * SUB + sub).astype(F32) if i < 2 else jnp.zeros((SUB, LANES), F32)
        rows[i][at] = jnp.where(own, unit, rows[i][at])
    scaled = []
    for it in range(2):
        shift = jnp.zeros((SUB, LANES), F32)
        scale = jnp.zeros((SUB, LANES), F32)
        for sl in range(0, SUB, 2):
            s = it * SUB + sl
            a = row_of(cols[s][it], sl)
            b = row_of(cols[s][it], sl + 1)
            c = row_of(cols[s + 1][it], sl + 1)
            det = a * c - b * b
            rdet = 1.0 / det
            ra = lax.rsqrt(a)
            ba = b * (ra * ra)
            rc = lax.rsqrt(c - b * ba)
            scale = jnp.where(sub == sl, ra, jnp.where(sub == sl + 1, rc, scale))
            shift = jnp.where(sub == sl + 1, ba, shift)
            begin = it if sl + 2 < SUB else it + 1
            m0, m1 = [None] * n_tiles, [None] * n_tiles
            for i in range(begin, n_tiles):
                u0, u1 = cols[s][i], cols[s + 1][i]
                m0[i] = (u0 * c - u1 * b) * rdet
                m1[i] = (u1 * a - u0 * b) * rdet
                if i == it:
                    m0[i] = jnp.where(sub > sl + 1, m0[i], 0.0)
                    m1[i] = jnp.where(sub > sl + 1, m1[i], 0.0)
            for j in range(s + 2, HALF):
                x0 = row_of(cols[s][j // SUB], j % SUB)
                x1 = row_of(cols[s + 1][j // SUB], j % SUB)
                for i in range(max(begin, j // SUB), n_tiles):
                    cols[j][i] = cols[j][i] - (m0[i] * x0 + m1[i] * x1)
            for t in range(n_lt):
                y0 = row_of(rows[it][t], sl)
                y1 = row_of(rows[it][t], sl + 1)
                for i in range(begin, n_tiles):
                    rows[i][t] = rows[i][t] - (m0[i] * y0 + m1[i] * y1)
        scaled.append([(r - shift * pltpu.roll(r, 1, 0)) * scale for r in rows[it]])
    return scaled, rows[2:]


def inverse_factor(w_ref, x_ref, n):
    n_lt = n // LANES
    lane = lax.broadcasted_iota(jnp.int32, (SUB, LANES), 1)
    for r in range(0, n, PANEL):
        rows = [[w_ref[r + i * SUB : r + (i + 1) * SUB, t * LANES : (t + 1) * LANES] for t in range(n_lt)] for i in range(PANEL // SUB)]
        upper, lower = eliminate(rows, r, 4)
        lower, _ = eliminate(lower, r + HALF, 2)
        at, off = r // LANES, r % LANES
        other = (lane >= off + HALF) & (lane < off + PANEL)
        for i in range(2):
            upper[i][at] = jnp.where(other, 0.0, upper[i][at])
        done = upper + lower
        for i in range(PANEL // SUB):
            for t in range(n_lt):
                tile = done[i][t]
                if t > at:
                    tile = jnp.zeros((SUB, LANES), F32)
                elif t == at:
                    tile = jnp.where(lane >= off + PANEL, 0.0, tile)
                x_ref[r + i * SUB : r + (i + 1) * SUB, t * LANES : (t + 1) * LANES] = tile
        nxt = r + PANEL
        if nxt == n:
            break
        whole = jnp.concatenate([jnp.concatenate(t, axis=1) for t in done], axis=0)
        base = nxt // LANES * LANES
        hi, lo = split2(whole)
        left = jnp.concatenate([hi, hi, lo], axis=0)[:, base:]
        right = jnp.concatenate([hi, lo, hi], axis=0)
        update = dot6(whole[:, base:], whole, TN)[nxt - base :, :]
        wide = lax.broadcasted_iota(jnp.int32, (n - nxt, n), 1)
        w_ref[nxt:, :] = jnp.where((wide >= r) & (wide < nxt), 0.0, w_ref[nxt:, :]) - update


def per_device_kernel(chunk, cols_n, table_ref, pivots_ref, panels_ref, schur_ref, w_ref, x_ref):
    row_start = lax.axis_index("row") * panels_ref.shape[0]
    col_start = lax.axis_index("col") * cols_n
    n_piv = w_ref.shape[0]
    n_tab = table_ref.shape[0]
    lane_ids = pivots_ref[...]
    ids = jnp.concatenate(
        [jnp.broadcast_to(lane_ids[i : i + 1, :].astype(F32), (LANES, LANES)).T for i in range(n_piv // LANES)], axis=0
    ).astype(jnp.int32)
    select = jnp.concatenate(
        [(ids // PER_ROW == t * LANES + lax.broadcasted_iota(jnp.int32, (n_piv, LANES), 1)).astype(BF16) for t in range(n_tab // LANES)],
        axis=1,
    )
    piv = unpack_points(table_ref[...], select, ids[:, :1] % PER_ROW)
    own = lax.broadcasted_iota(jnp.int32, (n_piv, n_piv), 0) == lax.broadcasted_iota(jnp.int32, (n_piv, n_piv), 1)
    w_ref[...] = exp_dist(piv, piv) + jnp.where(own, 0.1, 0.0)
    inverse_factor(w_ref, x_ref, n_piv)
    x_hi, x_lo = split2(x_ref[...])
    piv_row = jnp.concatenate([lane_ids[i : i + 1, :] for i in range(n_piv // LANES)], axis=1)

    def panel_of(start, count):
        pts = run_points(table_ref, start, count)
        ids_here = start + lax.broadcasted_iota(jnp.int32, (count, n_piv), 0)
        c = exp_dist(pts, piv) + jnp.where(ids_here == piv_row, 0.1, 0.0)
        c_hi, c_lo = split2(c)
        return pts, dot6(c, x_ref[...], NT)

    col_pts, col_panel = panel_of(col_start, cols_n)
    c_hi, c_lo = split2(col_panel)

    def one_chunk(at):
        start = row_start + at
        pts, panel = panel_of(start, chunk)
        panels_ref[pl.ds(at, chunk), :] = panel
        p_hi, p_lo = split2(panel)
        low = dot6(panel, col_panel, NT)
        ids_row = start + lax.broadcasted_iota(jnp.int32, (chunk, cols_n), 0)
        ids_col = col_start + lax.broadcasted_iota(jnp.int32, (chunk, cols_n), 1)
        schur_ref[pl.ds(at, chunk), :] = exp_dist(pts, col_pts) + jnp.where(ids_row == ids_col, 0.1, 0.0) - low

    n_rows = panels_ref.shape[0]
    if n_rows == chunk:
        one_chunk(0)
    else:

        @pl.loop(0, n_rows // chunk)
        def _(i):
            one_chunk(pl.multiple_of(i * chunk, chunk))


def per_device(points, pivots_first, pivots_second):
    per_dev = points.shape[1]
    n_row = lax.axis_size("row")
    n_col = lax.axis_size("col")
    rows_n = per_dev * n_col
    cols_n = per_dev * n_row
    n_piv = pivots_first.shape[0] + pivots_second.shape[0]
    packed = points.T.reshape(per_dev * DIM // LANES, LANES)
    table = lax.all_to_all(jnp.tile(packed, (n_row * n_col, 1)), ("row", "col"), 0, 0, tiled=True)
    pivots = jnp.concatenate([pivots_first, pivots_second]).reshape(n_piv // LANES, LANES)
    chunk = min(rows_n, 256)
    return pl.pallas_call(
        functools.partial(per_device_kernel, chunk, cols_n),
        out_shape=(jax.ShapeDtypeStruct((rows_n, n_piv), F32), jax.ShapeDtypeStruct((rows_n, cols_n), F32)),
        in_specs=[pl.BlockSpec(memory_space=pltpu.VMEM)] * 2,
        out_specs=(pl.BlockSpec(memory_space=pltpu.VMEM),) * 2,
        scratch_shapes=[pltpu.VMEM((n_piv, n_piv), F32)] * 2,
        name="pivoted_cholesky",
    )(table, pivots)


def solution(mesh):
    return jax.shard_map(
        per_device,
        mesh=mesh,
        in_specs=(P(None, ("row", "col")), P(), P()),
        out_specs=(P("row", None), P("row", "col")),
        check_vma=False,
    )
```

```python
import functools

import jax
import jax.numpy as jnp
from jax import lax
from jax.experimental import pallas as pl
from jax.experimental.pallas import tpu as pltpu
from jax.sharding import PartitionSpec as P

DIM = 16
LANES = 128
SUB = 8
HALF = 16
PANEL = 32
PER_ROW = LANES // DIM
VMEM_BYTES = 24 * 2**20
F32 = jnp.float32
BF16 = jnp.bfloat16
NN = (((1,), (0,)), ((), ()))
NT = (((1,), (1,)), ((), ()))
TN = (((0,), (0,)), ((), ()))


def dot(a, b, dims):
    return lax.dot_general(a, b, dims, preferred_element_type=F32)


def split3(a):
    hi = a.astype(BF16)
    rest = a - hi.astype(F32)
    mid = rest.astype(BF16)
    return hi, mid, (rest - mid.astype(F32)).astype(BF16)


def dot6(a, b, dims):
    a0, a1, a2 = split3(a)
    b0, b1, b2 = split3(b)
    return dot(a0, b0, dims) + ((dot(a0, b1, dims) + dot(a1, b0, dims)) + (dot(a1, b1, dims) + (dot(a0, b2, dims) + dot(a2, b0, dims))))

def exp_dist(left, right):
    left_sq = jnp.sum(left * left, axis=1, keepdims=True)
    ones = jnp.ones((SUB, DIM), F32)
    right_sq = lax.dot_general(ones, right * right, NT, precision=lax.Precision.HIGHEST, preferred_element_type=F32)[:1]
    inner = lax.dot_general(left, right, NT, precision=lax.Precision.HIGHEST, preferred_element_type=F32)
    return jnp.exp((left_sq + right_sq - 2.0 * inner) * (-1.0 / DIM))


def unpack_points(table, select, segment):
    n = segment.shape[0]
    lane = lax.broadcasted_iota(jnp.int32, (n, LANES), 1)
    keep = (lane // DIM) == segment
    fold = (lax.broadcasted_iota(jnp.int32, (LANES, DIM), 0) % DIM == lax.broadcasted_iota(jnp.int32, (LANES, DIM), 1)).astype(BF16)
    total = None
    for part in split3(table):
        row = dot(select, part, NN)
        x = dot(jnp.where(keep, row, 0.0).astype(BF16), fold, NN)
        total = x if total is None else total + x
    return total


def run_points(table_ref, start, count):
    rows = count // PER_ROW
    table = table_ref[pl.ds(pl.multiple_of(start // PER_ROW, SUB), rows), :]
    ids = lax.broadcasted_iota(jnp.int32, (count, rows), 0)
    select = (ids // PER_ROW == lax.broadcasted_iota(jnp.int32, (count, rows), 1)).astype(BF16)
    segment = lax.broadcasted_iota(jnp.int32, (count, 1), 0) % PER_ROW
    return unpack_points(table, select, segment)


def row_of(tile, s):
    return jnp.broadcast_to(tile[s : s + 1, :], (SUB, LANES))


def eliminate(rows, first_lane, n_tiles):
    sub = lax.broadcasted_iota(jnp.int32, (SUB, LANES), 0)
    lane = lax.broadcasted_iota(jnp.int32, (SUB, LANES), 1)
    at, off = first_lane // LANES, first_lane % LANES
    n_lt = len(rows[0])
    cols = [
        [
            jnp.broadcast_to(jnp.sum(jnp.where(lane == off + j, rows[i][at], 0.0), axis=1, keepdims=True), (SUB, LANES)) if i >= j // SUB else None
            for i in range(n_tiles)
        ]
        for j in range(HALF)
    ]
    own = (lane >= off) & (lane < off + HALF)
    for i in range(n_tiles):
        unit = (lane == off + i * SUB + sub).astype(F32) if i < HALF // SUB else jnp.zeros((SUB, LANES), F32)
        rows[i][at] = jnp.where(own, unit, rows[i][at])
    scaled = []
    for it in range(HALF // SUB):
        shift = jnp.zeros((SUB, LANES), F32)
        scale = jnp.zeros((SUB, LANES), F32)
        for sl in range(0, SUB, 2):
            s = it * SUB + sl
            a = row_of(cols[s][it], sl)
            b = row_of(cols[s][it], sl + 1)
            c = row_of(cols[s + 1][it], sl + 1)
            det = a * c - b * b
            rdet = 1.0 / det
            ra = lax.rsqrt(a)
            ba = b * (ra * ra)
            rc = lax.rsqrt(c - b * ba)
            scale = jnp.where(sub == sl, ra, jnp.where(sub == sl + 1, rc, scale))
            shift = jnp.where(sub == sl + 1, ba, shift)
            begin = it if sl + 2 < SUB else it + 1
            m0, m1 = [None] * n_tiles, [None] * n_tiles
            for i in range(begin, n_tiles):
                u0, u1 = cols[s][i], cols[s + 1][i]
                m0[i] = (u0 * c - u1 * b) * rdet
                m1[i] = (u1 * a - u0 * b) * rdet
                if i == it:
                    m0[i] = jnp.where(sub > sl + 1, m0[i], 0.0)
                    m1[i] = jnp.where(sub > sl + 1, m1[i], 0.0)
            for j in range(s + 2, HALF):
                x0 = row_of(cols[s][j // SUB], j % SUB)
                x1 = row_of(cols[s + 1][j // SUB], j % SUB)
                for i in range(max(begin, j // SUB), n_tiles):
                    cols[j][i] = cols[j][i] - (m0[i] * x0 + m1[i] * x1)
            for t in range(n_lt):
                y0 = row_of(rows[it][t], sl)
                y1 = row_of(rows[it][t], sl + 1)
                for i in range(begin, n_tiles):
                    rows[i][t] = rows[i][t] - (m0[i] * y0 + m1[i] * y1)
        scaled.append([(r - shift * pltpu.roll(r, 1, 0)) * scale for r in rows[it]])
    return scaled, rows[HALF // SUB :]


def inverse_factor(w_ref, x_ref, n):
    n_lt = n // LANES
    lane = lax.broadcasted_iota(jnp.int32, (SUB, LANES), 1)
    for r in range(0, n, PANEL):
        rows = [[w_ref[r + i * SUB : r + (i + 1) * SUB, t * LANES : (t + 1) * LANES] for t in range(n_lt)] for i in range(PANEL // SUB)]
        at, off = r // LANES, r % LANES
        done = []
        for begin in range(0, PANEL, HALF):
            upper, rows = eliminate(rows, r + begin, len(rows))
            other = (lane >= off + begin + HALF) & (lane < off + PANEL)
            for tiles in upper:
                tiles[at] = jnp.where(other, 0.0, tiles[at])
            done += upper
        for i in range(PANEL // SUB):
            for t in range(n_lt):
                tile = done[i][t]
                if t > at:
                    tile = jnp.zeros((SUB, LANES), F32)
                elif t == at:
                    tile = jnp.where(lane >= off + PANEL, 0.0, tile)
                x_ref[r + i * SUB : r + (i + 1) * SUB, t * LANES : (t + 1) * LANES] = tile
        nxt = r + PANEL
        if nxt == n:
            break
        whole = jnp.concatenate([jnp.concatenate(t, axis=1) for t in done], axis=0)
        base = nxt // LANES * LANES
        r0, r1, r2 = split3(whole)
        left = jnp.concatenate([r0, r0, r1, r1, r0, r2], axis=0)[:, base:].T
        right = jnp.concatenate([r0, r1, r0, r1, r2, r0], axis=0)
        wide = lax.broadcasted_iota(jnp.int32, (PANEL, n), 1)
        mid = nxt + PANEL
        update = dot(left[nxt - base : mid - base, :], right, NN)
        w_ref[nxt:mid, :] = jnp.where((wide >= r) & (wide < nxt), 0.0, w_ref[nxt:mid, :]) - update
        if mid < n:
            wide = lax.broadcasted_iota(jnp.int32, (n - mid, n), 1)
            update = dot(left[mid - base :, :], right, NN)
            w_ref[mid:, :] = jnp.where((wide >= r) & (wide < nxt), 0.0, w_ref[mid:, :]) - update


def per_device_kernel(chunk, cols_n, table_ref, pivots_ref, panels_ref, schur_ref, w_ref, x_ref):
    row_start = lax.axis_index("row") * panels_ref.shape[0]
    col_start = lax.axis_index("col") * cols_n
    n_piv = w_ref.shape[0]
    n_tab = table_ref.shape[0]
    n_rows = panels_ref.shape[0]
    lane_ids = pivots_ref[...]
    ids = jnp.concatenate(
        [jnp.broadcast_to(lane_ids[i : i + 1, :].astype(F32), (LANES, LANES)).T for i in range(n_piv // LANES)], axis=0
    ).astype(jnp.int32)
    select = jnp.concatenate(
        [(ids // PER_ROW == t * LANES + lax.broadcasted_iota(jnp.int32, (n_piv, LANES), 1)).astype(BF16) for t in range(n_tab // LANES)],
        axis=1,
    )
    piv = unpack_points(table_ref[...], select, ids[:, :1] % PER_ROW)
    own = lax.broadcasted_iota(jnp.int32, (n_piv, n_piv), 0) == lax.broadcasted_iota(jnp.int32, (n_piv, n_piv), 1)
    w_ref[...] = exp_dist(piv, piv) + jnp.where(own, 0.1, 0.0)
    piv_row = jnp.concatenate([lane_ids[i : i + 1, :] for i in range(n_piv // LANES)], axis=1)

    def columns_of(start, count):
        pts = run_points(table_ref, start, count)
        ids_here = start + lax.broadcasted_iota(jnp.int32, (count, n_piv), 0)
        return pts, exp_dist(pts, piv) + jnp.where(ids_here == piv_row, 0.1, 0.0)

    col_pts, col_columns = columns_of(col_start, cols_n)

    def prepare(at):
        start = row_start + at
        pts, columns = columns_of(start, chunk)
        ids_row = start + lax.broadcasted_iota(jnp.int32, (chunk, cols_n), 0)
        ids_col = col_start + lax.broadcasted_iota(jnp.int32, (chunk, cols_n), 1)
        return columns, exp_dist(pts, col_pts) + jnp.where(ids_row == ids_col, 0.1, 0.0)

    def finish(at, columns, k_cols, x, col_panel):
        panel = dot6(columns, x, NT)
        panels_ref[pl.ds(at, chunk), :] = panel
        schur_ref[pl.ds(at, chunk), :] = k_cols - dot6(panel, col_panel, NT)

    if n_rows == chunk:
        inverse_factor(w_ref, x_ref, n_piv)
        columns, k_cols = prepare(0)
        x = x_ref[...]
        both = dot6(jnp.concatenate([columns, col_columns], axis=0), x, NT)
        panels_ref[...] = both[:chunk]
        schur_ref[...] = k_cols - dot6(both[:chunk], both[chunk:], NT)
    else:
        inverse_factor(w_ref, x_ref, n_piv)
        col_panel = dot6(col_columns, x_ref[...], NT)

        @pl.loop(0, n_rows // chunk)
        def _(i):
            at = pl.multiple_of(i * chunk, chunk)
            columns, k_cols = prepare(at)
            finish(at, columns, k_cols, x_ref[...], col_panel)


def per_device(points, pivots_first, pivots_second):
    per_dev = points.shape[1]
    n_row = lax.axis_size("row")
    n_col = lax.axis_size("col")
    rows_n = per_dev * n_col
    cols_n = per_dev * n_row
    n_piv = pivots_first.shape[0] + pivots_second.shape[0]
    packed = points.T.reshape(per_dev * DIM // LANES, LANES)
    table = lax.all_to_all(jnp.tile(packed, (n_row * n_col, 1)), ("row", "col"), 0, 0, tiled=True)
    pivots = jnp.concatenate([pivots_first, pivots_second]).reshape(n_piv // LANES, LANES)
    chunk = min(rows_n, 256)
    return pl.pallas_call(
        functools.partial(per_device_kernel, chunk, cols_n),
        out_shape=(jax.ShapeDtypeStruct((rows_n, n_piv), F32), jax.ShapeDtypeStruct((rows_n, cols_n), F32)),
        in_specs=[pl.BlockSpec(memory_space=pltpu.VMEM)] * 2,
        out_specs=(pl.BlockSpec(memory_space=pltpu.VMEM),) * 2,
        scratch_shapes=[pltpu.VMEM((n_piv, n_piv), F32)] * 2,
        compiler_params=pltpu.CompilerParams(vmem_limit_bytes=VMEM_BYTES),
        name="pivoted_cholesky",
    )(table, pivots)


def solution(mesh):
    return jax.shard_map(
        per_device,
        mesh=mesh,
        in_specs=(P(None, ("row", "col")), P(), P()),
        out_specs=(P("row", None), P("row", "col")),
        check_vma=False,
    )
```

```python
import functools

import jax
import jax.numpy as jnp
from jax import lax
from jax.experimental import pallas as pl
from jax.experimental.pallas import tpu as pltpu
from jax.sharding import PartitionSpec as P

DIM = 16
LANES = 128
SUB = 8
BLOCK = 16
PER_ROW = LANES // DIM
VMEM_BYTES = 24 * 2**20
F32 = jnp.float32
BF16 = jnp.bfloat16
NN = (((1,), (0,)), ((), ()))
NT = (((1,), (1,)), ((), ()))
TN = (((0,), (0,)), ((), ()))
LEFT = (0, 0, 1, 1, 0, 2)
RIGHT = (0, 1, 0, 1, 2, 0)
NORM = len(LEFT) * DIM


def iota(shape, axis):
    return lax.broadcasted_iota(jnp.int32, shape, axis)


def dot(a, b, dims):
    return lax.dot_general(a, b, dims, preferred_element_type=F32)


def split3(a):
    hi = a.astype(BF16)
    rest = a - hi.astype(F32)
    mid = rest.astype(BF16)
    return hi, mid, (rest - mid.astype(F32)).astype(BF16)


def dot6(a, b, dims):
    p = [dot(a[i], b[j], dims) for i, j in zip(LEFT, RIGHT)]
    return p[0] + ((p[1] + p[2]) + ((p[3] + p[4]) + p[5]))


def pack_kernel(points_in, first_in, second_in, table_ref, select_ref, keep_ref, ids_ref, place_ref, points_ref, first_ref, second_ref, sems):
    copies = [
        pltpu.make_async_copy(src, dst, sems.at[i])
        for i, (src, dst) in enumerate(((points_in, points_ref), (first_in, first_ref), (second_in, second_ref)))
    ]
    for copy in copies:
        copy.start()
    lane = iota((LANES, LANES), 1)
    same = lane % DIM == iota((LANES, LANES), 0) % DIM
    for third in range(3):
        for side, pattern in enumerate((LEFT, RIGHT)):
            hit = None
            for group, which in enumerate(pattern):
                if which == third:
                    here = lane // DIM == group
                    hit = here if hit is None else hit | here
            place_ref[third * LANES : (third + 1) * LANES, side * LANES : (side + 1) * LANES] = (same & hit).astype(BF16)
        place_ref[third * LANES : (third + 1) * LANES, 2 * LANES :] = (same & (lane < DIM)).astype(BF16)
    for copy in copies:
        copy.wait()
    n = points_ref.shape[1]
    spread_to = (iota((DIM, LANES), 1) % DIM == iota((DIM, LANES), 0)).astype(BF16)
    wide = None
    for part in split3(points_ref[...]):
        x = dot(part, spread_to, TN)
        wide = x if wide is None else wide + x
    wide = jnp.where(iota((n, LANES), 1) // DIM == iota((n, LANES), 0) % PER_ROW, wide, 0.0)
    block = jnp.concatenate([jnp.sum(wide[i : i + PER_ROW, :], axis=0, keepdims=True) for i in range(0, n, PER_ROW)], axis=0)
    table_ref[...] = jnp.concatenate([block] * (table_ref.shape[0] // block.shape[0]), axis=0)
    at = 0
    for ref in (first_ref, second_ref):
        count = ref.shape[1]
        ids_ref[:, at : at + count] = jnp.broadcast_to(ref[...], (SUB, count))
        ids = jnp.broadcast_to(ref[...].astype(F32), (LANES, count)).T.astype(jnp.int32)
        for t in range(0, table_ref.shape[0], LANES):
            select_ref[at : at + count, t : t + LANES] = (ids // PER_ROW == t + iota((count, LANES), 1)).astype(BF16)
        keep_ref[at : at + count, :] = (ids % PER_ROW == iota((count, LANES), 1) // DIM).astype(F32)
        at += count


def features_of(select, table, keep, place):
    n = select.shape[0]
    thirds = jnp.concatenate([(dot(select, part, NN) * keep).astype(BF16) for part in table], axis=1)
    both = dot(thirds, place, NN)
    x = both[:, 2 * LANES :]
    norm = jnp.sum(x * x, axis=1, keepdims=True)
    right = both[:, LANES : 2 * LANES]
    for i, part in enumerate(split3(jnp.broadcast_to(norm, (n, LANES)))):
        right = jnp.where(iota((n, LANES), 1) == NORM + i, part.astype(F32), right)
    return both[:, :LANES], right.astype(BF16), norm


def rbf(left, norm, right):
    n = left.shape[0]
    lane = iota((2 * SUB, LANES), 1)
    ones = ((lane >= NORM) & (lane < NORM + 3)).astype(BF16)
    lead = iota((n, LANES), 1) < DIM
    both = dot(jnp.concatenate([ones, jnp.where(lead, left, 0.0).astype(BF16), jnp.where(lead, 0.0, left).astype(BF16)], axis=0), right, NT)
    inner = both[2 * SUB : 2 * SUB + n] + both[2 * SUB + n :]
    return jnp.exp((norm + both[:1] - 2.0 * inner) * (-1.0 / DIM))


def row_of(tile, s):
    return jnp.broadcast_to(tile[s : s + 1, :], (SUB, LANES))


def spread(x):
    return jnp.broadcast_to(jnp.sum(x, axis=1, keepdims=True), (SUB, LANES))


def eliminate(rows, first_lane, more):
    sub = lax.broadcasted_iota(jnp.int32, (SUB, LANES), 0)
    lane = lax.broadcasted_iota(jnp.int32, (SUB, LANES), 1)
    at, off = first_lane // LANES, first_lane % LANES
    at2, off2 = (first_lane + BLOCK) // LANES, (first_lane + BLOCK) % LANES
    n_lt = len(rows[0])
    n_cur = BLOCK // SUB
    n_tiles = 2 * n_cur if more else n_cur
    cols = []
    for j in range(BLOCK):
        tiles = [spread(jnp.where(lane == off + j, rows[i][at], 0.0)) if i >= j // SUB else None for i in range(n_cur)]
        if more:
            row = row_of(rows[j // SUB][at2], j % SUB)
            tiles += [spread(jnp.where(lane == off2 + i * SUB + sub, row, 0.0)) for i in range(n_cur)]
        cols.append(tiles)
    own = (lane >= off) & (lane < off + BLOCK)
    rows = [list(r) for r in rows]
    for i in range(n_cur):
        rows[i][at] = jnp.where(own, (lane == off + i * SUB + sub).astype(F32), rows[i][at])
    if more:
        rows += [[jnp.zeros((SUB, LANES), F32) for _ in range(n_lt)] for _ in range(n_cur)]
    scaled = []
    for it in range(n_cur):
        shift = jnp.zeros((SUB, LANES), F32)
        scale = jnp.zeros((SUB, LANES), F32)
        for sl in range(0, SUB, 2):
            s = it * SUB + sl
            a = row_of(cols[s][it], sl)
            b = row_of(cols[s][it], sl + 1)
            c = row_of(cols[s + 1][it], sl + 1)
            det = a * c - b * b
            rdet = 1.0 / det
            ra = lax.rsqrt(a)
            ba = b * (ra * ra)
            rc = lax.rsqrt(c - b * ba)
            scale = jnp.where(sub == sl, ra, jnp.where(sub == sl + 1, rc, scale))
            shift = jnp.where(sub == sl + 1, ba, shift)
            begin = it if sl + 2 < SUB else it + 1
            m0, m1 = [None] * n_tiles, [None] * n_tiles
            for i in range(begin, n_tiles):
                u0, u1 = cols[s][i], cols[s + 1][i]
                m0[i] = (u0 * c - u1 * b) * rdet
                m1[i] = (u1 * a - u0 * b) * rdet
                if i == it:
                    m0[i] = jnp.where(sub > sl + 1, m0[i], 0.0)
                    m1[i] = jnp.where(sub > sl + 1, m1[i], 0.0)
            for j in range(s + 2, BLOCK):
                x0 = row_of(cols[s][j // SUB], j % SUB)
                x1 = row_of(cols[s + 1][j // SUB], j % SUB)
                for i in range(max(begin, j // SUB), n_tiles):
                    cols[j][i] = cols[j][i] - (m0[i] * x0 + m1[i] * x1)
            for t in range(n_lt):
                y0 = row_of(rows[it][t], sl)
                y1 = row_of(rows[it][t], sl + 1)
                for i in range(begin, n_tiles):
                    rows[i][t] = rows[i][t] - (m0[i] * y0 + m1[i] * y1)
        scaled.append([(r - shift * pltpu.roll(r, 1, 0)) * scale for r in rows[it]])
    return scaled, rows[n_cur:]


def inverse_factor(w_ref, x_refs, n, hooks):
    n_lt = n // LANES
    n_cur = BLOCK // SUB
    lane = iota((SUB, LANES), 1)

    def load(i, t):
        return w_ref[i * SUB : (i + 1) * SUB, t * LANES : (t + 1) * LANES]

    rows = [[load(i, t) for t in range(n_lt)] for i in range(n_cur)]
    for r in range(0, n, BLOCK):
        nxt = r + BLOCK
        at, off = r // LANES, r % LANES
        own = (lane >= off) & (lane < off + BLOCK)
        done, below = eliminate(rows, r, nxt < n)
        if nxt < n:
            rows = []
            for i in range(n_cur):
                tiles = [load(nxt // SUB + i, t) for t in range(n_lt)]
                tiles[at] = jnp.where(own, 0.0, tiles[at])
                rows.append([tile + more for tile, more in zip(tiles, below[i])])
        whole = jnp.concatenate([jnp.concatenate(t, axis=1) for t in done], axis=0)
        thirds = split3(whole)
        width = (at + 1) * LANES
        inside = iota((BLOCK, width), 1) < nxt
        for x_ref, part in zip(x_refs, thirds):
            x_ref[r:nxt, :width] = jnp.where(inside, part[:, :width].astype(F32), 0.0).astype(BF16)
        rest = nxt + BLOCK
        if rest < n:
            base = rest // LANES * LANES
            left = jnp.concatenate([thirds[i] for i in LEFT], axis=0)[:, base:].T
            right = jnp.concatenate([thirds[i] for i in RIGHT], axis=0)
            cuts = [rest, rest + BLOCK, n] if rest + BLOCK < n else [rest, n]
            for begin, end in zip(cuts, cuts[1:]):
                update = dot(left[begin - base : end - base, :], right, NN)
                wide = iota((end - begin, n), 1)
                w_ref[begin:end, :] = jnp.where((wide >= r) & (wide < nxt), 0.0, w_ref[begin:end, :]) - update
        for hook in hooks.get(nxt, ()):
            hook()


def per_device_kernel(
    table_ref, select_ref, keep_ref, ids_ref, place_ref, panels_out, schur_out,
    w_ref, x_refs, panels_ref, schur_ref, cols_right_ref, col_thirds, row_thirds, col_panel, row_panel, sems,
):
    n_rows, n_piv = panels_ref.shape
    cols_n = schur_ref.shape[1]
    chunk = row_thirds.shape[1]
    row_start = lax.axis_index("row") * n_rows
    col_start = lax.axis_index("col") * cols_n
    half = n_piv // 2
    place = place_ref[...]
    left, right, norm = features_of(select_ref[...], split3(table_ref[...]), keep_ref[...], place)
    own = iota((n_piv, n_piv), 0) == iota((n_piv, n_piv), 1)
    w_ref[...] = rbf(left, norm, right) + jnp.where(own, 0.1, 0.0)

    def run_features(start, count):
        rows = count // PER_ROW
        table = split3(table_ref[pl.ds(pl.multiple_of(start // PER_ROW, SUB), rows), :])
        select = (iota((count, rows), 0) // PER_ROW == iota((count, rows), 1)).astype(BF16)
        keep = (iota((count, LANES), 0) % PER_ROW == iota((count, LANES), 1) // DIM).astype(F32)
        return features_of(select, table, keep, place)

    def columns(out, at, start, count, side, norm):
        ids = start + iota((count, n_piv), 0)
        c = rbf(side, norm, right) + jnp.where(ids == ids_ref[:1, :], 0.1, 0.0)
        for i, part in enumerate(split3(c)):
            out[i, at : at + count, :] = part

    def col_columns():
        side, cols_right, norm = run_features(col_start, cols_n)
        cols_right_ref[...] = cols_right
        columns(col_thirds, 0, col_start, cols_n, side, norm)

    def row_columns(at, part, count):
        start = row_start + at + part
        side, _, norm = run_features(start, count)
        columns(row_thirds, part, start, count, side, norm)
        ids_row = start + iota((count, cols_n), 0)
        ids_col = col_start + iota((count, cols_n), 1)
        schur_ref[pl.ds(at + part, count), :] = rbf(side, norm, cols_right_ref[...]) + jnp.where(ids_row == ids_col, 0.1, 0.0)

    def panel_half(c_thirds, k):
        upto = (k + 1) * half
        return dot6([c_thirds[i, :, :upto] for i in range(3)], [x[k * half : upto, :upto] for x in x_refs], NT)

    def col_half(k):
        for i, part in enumerate(split3(panel_half(col_thirds, k))):
            col_panel[i, :, k * half : (k + 1) * half] = part

    def row_half(at, k):
        panel = panel_half(row_thirds, k)
        panels_ref[pl.ds(at, chunk), k * half : (k + 1) * half] = panel
        for i, part in enumerate(split3(panel)):
            row_panel[i, :, k * half : (k + 1) * half] = part

    def schur_half(at, k):
        here = slice(k * half, (k + 1) * half)
        low = dot6([row_panel[i, :, here] for i in range(3)], [col_panel[i, :, here] for i in range(3)], NT)
        schur_ref[pl.ds(at, chunk), :] = schur_ref[pl.ds(at, chunk), :] - low

    panel_copies = [
        pltpu.make_async_copy(
            panels_ref.at[:, k * half : (k + 1) * half], panels_out.at[:, k * half : (k + 1) * half], sems.at[k]
        )
        for k in range(2)
    ]
    schur_copy = pltpu.make_async_copy(schur_ref, schur_out, sems.at[2])
    if n_rows == chunk:
        q = chunk // 2
        hooks = {
            2 * BLOCK: [col_columns],
            4 * BLOCK: [lambda: row_columns(0, 0, q)],
            6 * BLOCK: [lambda: row_columns(0, q, q)],
            9 * BLOCK: [lambda: row_half(0, 0), panel_copies[0].start],
            11 * BLOCK: [lambda: col_half(0)],
            13 * BLOCK: [lambda: schur_half(0, 0)],
        }
        inverse_factor(w_ref, x_refs, n_piv, hooks)
        row_half(0, 1)
        panel_copies[1].start()
        col_half(1)
        schur_half(0, 1)
        schur_copy.start()
    else:
        inverse_factor(w_ref, x_refs, n_piv, {})
        col_columns()
        col_half(0)
        col_half(1)

        @pl.loop(0, n_rows // chunk)
        def _(i):
            at = pl.multiple_of(i * chunk, chunk)
            row_columns(at, 0, chunk)
            for k in range(2):
                row_half(at, k)
                schur_half(at, k)

        for copy in panel_copies:
            copy.start()
        schur_copy.start()
    for copy in panel_copies:
        copy.wait()
    schur_copy.wait()


def per_device(points, pivots_first, pivots_second):
    per_dev = points.shape[1]
    n_row = lax.axis_size("row")
    n_col = lax.axis_size("col")
    rows_n = per_dev * n_col
    cols_n = per_dev * n_row
    n_piv = pivots_first.shape[0] + pivots_second.shape[0]
    n_tab = n_row * n_col * per_dev * DIM // LANES
    vmem = pl.BlockSpec(memory_space=pltpu.VMEM)
    params = pltpu.CompilerParams(vmem_limit_bytes=VMEM_BYTES)
    copies, *found = pl.pallas_call(
        pack_kernel,
        out_shape=(
            jax.ShapeDtypeStruct((n_tab, LANES), F32),
            jax.ShapeDtypeStruct((n_piv, n_tab), BF16),
            jax.ShapeDtypeStruct((n_piv, LANES), F32),
            jax.ShapeDtypeStruct((SUB, n_piv), jnp.int32),
            jax.ShapeDtypeStruct((3 * LANES, 3 * LANES), BF16),
        ),
        in_specs=[pl.BlockSpec(memory_space=pltpu.HBM)] * 3,
        out_specs=(vmem,) * 5,
        scratch_shapes=[
            pltpu.VMEM((DIM, per_dev), F32),
            pltpu.VMEM((1, pivots_first.shape[0]), jnp.int32),
            pltpu.VMEM((1, pivots_second.shape[0]), jnp.int32),
            pltpu.SemaphoreType.DMA((3,)),
        ],
        compiler_params=params,
        name="pack",
    )(*(pltpu.with_memory_space_constraint(x, pltpu.HBM) for x in (points, pivots_first[None, :], pivots_second[None, :])))
    table = lax.all_to_all(copies, ("row", "col"), 0, 0, tiled=True)
    table, *found = lax.optimization_barrier((table, *found))
    chunk = min(rows_n, 256)
    return pl.pallas_call(
        per_device_kernel,
        out_shape=(jax.ShapeDtypeStruct((rows_n, n_piv), F32), jax.ShapeDtypeStruct((rows_n, cols_n), F32)),
        in_specs=[vmem] * 5,
        out_specs=(pl.BlockSpec(memory_space=pl.ANY),) * 2,
        scratch_shapes=[
            pltpu.VMEM((n_piv, n_piv), F32),
            [pltpu.VMEM((n_piv, n_piv), BF16)] * 3,
            pltpu.VMEM((rows_n, n_piv), F32),
            pltpu.VMEM((rows_n, cols_n), F32),
            pltpu.VMEM((cols_n, LANES), BF16),
            pltpu.VMEM((3, cols_n, n_piv), BF16),
            pltpu.VMEM((3, chunk, n_piv), BF16),
            pltpu.VMEM((3, cols_n, n_piv), BF16),
            pltpu.VMEM((3, chunk, n_piv), BF16),
            pltpu.SemaphoreType.DMA((3,)),
        ],
        compiler_params=params,
        name="pivoted_cholesky",
    )(table, *found)


def solution(mesh):
    return jax.shard_map(
        per_device,
        mesh=mesh,
        in_specs=(P(None, ("row", "col")), P(), P()),
        out_specs=(P("row", None), P("row", "col")),
        check_vma=False,
    )
```

```python
import functools

import jax
import jax.numpy as jnp
from jax import lax
from jax.experimental import pallas as pl
from jax.experimental.pallas import tpu as pltpu
from jax.sharding import PartitionSpec as P

DIM = 16
LANES = 128
SUB = 8
BLOCK = 16
PER_ROW = LANES // DIM
VMEM_BYTES = 24 * 2**20
F32 = jnp.float32
BF16 = jnp.bfloat16
NN = (((1,), (0,)), ((), ()))
NT = (((1,), (1,)), ((), ()))
TN = (((0,), (0,)), ((), ()))
LEFT = (0, 0, 1, 1, 0, 2)
RIGHT = (0, 1, 0, 1, 2, 0)
NORM = len(LEFT) * DIM


def iota(shape, axis):
    return lax.broadcasted_iota(jnp.int32, shape, axis)


def dot(a, b, dims):
    return lax.dot_general(a, b, dims, preferred_element_type=F32)


def split3(a):
    hi = a.astype(BF16)
    rest = a - hi.astype(F32)
    mid = rest.astype(BF16)
    return hi, mid, (rest - mid.astype(F32)).astype(BF16)


def dot6(a, b):
    n = b[0].shape[0]
    wide = dot(
        jnp.concatenate([a[0], a[1]], axis=1),
        jnp.concatenate([jnp.concatenate([b[0], b[0]], axis=1), jnp.concatenate([b[1], b[1]], axis=1)], axis=0),
        NT,
    )
    rest = dot(jnp.concatenate([a[0], a[2]], axis=1), jnp.concatenate([b[2], b[0]], axis=1), NT)
    return wide[:, :n] + (wide[:, n:] + rest)


def pack_kernel(points_in, first_in, second_in, table_ref, select_ref, keep_ref, ids_ref, place_ref, points_ref, first_ref, second_ref, sems):
    copies = [
        pltpu.make_async_copy(src, dst, sems.at[i])
        for i, (src, dst) in enumerate(((points_in, points_ref), (first_in, first_ref), (second_in, second_ref)))
    ]
    for copy in copies:
        copy.start()
    lane = iota((LANES, LANES), 1)
    same = lane % DIM == iota((LANES, LANES), 0) % DIM
    for third in range(3):
        for side, pattern in enumerate((LEFT, RIGHT)):
            hit = None
            for group, which in enumerate(pattern):
                if which == third:
                    here = lane // DIM == group
                    hit = here if hit is None else hit | here
            place_ref[third * LANES : (third + 1) * LANES, side * LANES : (side + 1) * LANES] = (same & hit).astype(BF16)
        place_ref[third * LANES : (third + 1) * LANES, 2 * LANES :] = (same & (lane < DIM)).astype(BF16)
    for copy in copies:
        copy.wait()
    n = points_ref.shape[1]
    spread_to = (iota((DIM, LANES), 1) % DIM == iota((DIM, LANES), 0)).astype(BF16)
    wide = None
    for part in split3(points_ref[...]):
        x = dot(part, spread_to, TN)
        wide = x if wide is None else wide + x
    wide = jnp.where(iota((n, LANES), 1) // DIM == iota((n, LANES), 0) % PER_ROW, wide, 0.0)
    block = jnp.concatenate([jnp.sum(wide[i : i + PER_ROW, :], axis=0, keepdims=True) for i in range(0, n, PER_ROW)], axis=0)
    table_ref[...] = jnp.concatenate([block] * (table_ref.shape[0] // block.shape[0]), axis=0)
    at = 0
    for ref in (first_ref, second_ref):
        count = ref.shape[1]
        ids_ref[:, at : at + count] = jnp.broadcast_to(ref[...], (SUB, count))
        ids = jnp.broadcast_to(ref[...].astype(F32), (LANES, count)).T.astype(jnp.int32)
        for t in range(0, table_ref.shape[0], LANES):
            select_ref[at : at + count, t : t + LANES] = (ids // PER_ROW == t + iota((count, LANES), 1)).astype(BF16)
        keep_ref[at : at + count, :] = (ids % PER_ROW == iota((count, LANES), 1) // DIM).astype(F32)
        at += count


def features_of(select, table, keep, place):
    n = select.shape[0]
    thirds = jnp.concatenate([(dot(select, part, NN) * keep).astype(BF16) for part in table], axis=1)
    both = dot(thirds, place, NN)
    x = both[:, 2 * LANES :]
    norm = jnp.sum(x * x, axis=1, keepdims=True)
    right = both[:, LANES : 2 * LANES]
    for i, part in enumerate(split3(jnp.broadcast_to(norm, (n, LANES)))):
        right = jnp.where(iota((n, LANES), 1) == NORM + i, part.astype(F32), right)
    return both[:, :LANES], right.astype(BF16), norm


def rbf(left, norm, right):
    n = left.shape[0]
    lane = iota((2 * SUB, LANES), 1)
    ones = ((lane >= NORM) & (lane < NORM + 3)).astype(BF16)
    lead = iota((n, LANES), 1) < DIM
    both = dot(jnp.concatenate([ones, jnp.where(lead, left, 0.0).astype(BF16), jnp.where(lead, 0.0, left).astype(BF16)], axis=0), right, NT)
    inner = both[2 * SUB : 2 * SUB + n] + both[2 * SUB + n :]
    return jnp.exp((norm + both[:1] - 2.0 * inner) * (-1.0 / DIM))


def row_of(tile, s):
    return jnp.broadcast_to(tile[s : s + 1, :], (SUB, LANES))


def spread(x):
    return jnp.broadcast_to(jnp.sum(x, axis=1, keepdims=True), (SUB, LANES))


def eliminate(rows, first_lane, more):
    sub = lax.broadcasted_iota(jnp.int32, (SUB, LANES), 0)
    lane = lax.broadcasted_iota(jnp.int32, (SUB, LANES), 1)
    at, off = first_lane // LANES, first_lane % LANES
    at2, off2 = (first_lane + BLOCK) // LANES, (first_lane + BLOCK) % LANES
    n_lt = len(rows[0])
    n_cur = BLOCK // SUB
    n_tiles = 2 * n_cur if more else n_cur
    cols = [
        [spread(jnp.where(lane == off + j, rows[i][at], 0.0)) if i >= j // SUB else None for i in range(n_cur)] for j in range(BLOCK)
    ]
    if more:
        for j in range(BLOCK):
            row = row_of(rows[j // SUB][at2], j % SUB)
            cols[j] += [spread(jnp.where(lane == off2 + i * SUB + sub, row, 0.0)) for i in range(n_cur)]
    own = (lane >= off) & (lane < off + BLOCK)
    rows = [list(r) for r in rows]
    for i in range(n_cur):
        rows[i][at] = jnp.where(own, (lane == off + i * SUB + sub).astype(F32), rows[i][at])
    if more:
        rows += [[jnp.zeros((SUB, LANES), F32) for _ in range(n_lt)] for _ in range(n_cur)]
    scaled = []
    for it in range(n_cur):
        shift = jnp.zeros((SUB, LANES), F32)
        scale = jnp.zeros((SUB, LANES), F32)
        for sl in range(0, SUB, 2):
            s = it * SUB + sl
            a = row_of(cols[s][it], sl)
            b = row_of(cols[s][it], sl + 1)
            c = row_of(cols[s + 1][it], sl + 1)
            det = a * c - b * b
            rdet = 1.0 / det
            ra = lax.rsqrt(a)
            ba = b * (ra * ra)
            rc = lax.rsqrt(c - b * ba)
            scale = jnp.where(sub == sl, ra, jnp.where(sub == sl + 1, rc, scale))
            shift = jnp.where(sub == sl + 1, ba, shift)
            begin = it if sl + 2 < SUB else it + 1
            m0, m1 = [None] * n_tiles, [None] * n_tiles
            for i in range(begin, n_tiles):
                u0, u1 = cols[s][i], cols[s + 1][i]
                m0[i] = (u0 * c - u1 * b) * rdet
                m1[i] = (u1 * a - u0 * b) * rdet
                if i == it:
                    m0[i] = jnp.where(sub > sl + 1, m0[i], 0.0)
                    m1[i] = jnp.where(sub > sl + 1, m1[i], 0.0)
            for j in range(s + 2, BLOCK):
                x0 = row_of(cols[s][j // SUB], j % SUB)
                x1 = row_of(cols[s + 1][j // SUB], j % SUB)
                for i in range(max(begin, j // SUB), n_tiles):
                    cols[j][i] = cols[j][i] - (m0[i] * x0 + m1[i] * x1)
            for t in range(n_lt):
                y0 = row_of(rows[it][t], sl)
                y1 = row_of(rows[it][t], sl + 1)
                for i in range(begin, n_tiles):
                    rows[i][t] = rows[i][t] - (m0[i] * y0 + m1[i] * y1)
        scaled.append([(r - shift * pltpu.roll(r, 1, 0)) * scale for r in rows[it]])
    return scaled, rows[n_cur:]


def inverse_factor(w_ref, x_refs, n, hooks):
    n_lt = n // LANES
    n_cur = BLOCK // SUB
    lane = iota((SUB, LANES), 1)

    def load(i, t):
        return w_ref[i * SUB : (i + 1) * SUB, t * LANES : (t + 1) * LANES]

    rows = [[load(i, t) for t in range(n_lt)] for i in range(n_cur)]
    for r in range(0, n, BLOCK):
        nxt = r + BLOCK
        at, off = r // LANES, r % LANES
        own = (lane >= off) & (lane < off + BLOCK)
        done, below = eliminate(rows, r, nxt < n)
        if nxt < n:
            rows = []
            for i in range(n_cur):
                tiles = [load(nxt // SUB + i, t) for t in range(n_lt)]
                tiles[at] = jnp.where(own, 0.0, tiles[at])
                rows.append([tile + more for tile, more in zip(tiles, below[i])])
        whole = jnp.concatenate([jnp.concatenate(t, axis=1) for t in done], axis=0)
        thirds = split3(whole)
        width = (at + 1) * LANES
        inside = iota((BLOCK, width), 1) < nxt
        for x_ref, part in zip(x_refs, thirds):
            x_ref[r:nxt, :width] = jnp.where(inside, part[:, :width].astype(F32), 0.0).astype(BF16)
        rest = nxt + BLOCK
        if rest < n:
            base = rest // LANES * LANES
            left = jnp.concatenate([thirds[i] for i in LEFT], axis=0)[:, base:].T
            right = jnp.concatenate([thirds[i] for i in RIGHT], axis=0)
            cuts = [rest, rest + BLOCK, n] if rest + BLOCK < n else [rest, n]
            for begin, end in zip(cuts, cuts[1:]):
                update = dot(left[begin - base : end - base, :], right, NN)
                wide = iota((end - begin, n), 1)
                w_ref[begin:end, :] = jnp.where((wide >= r) & (wide < nxt), 0.0, w_ref[begin:end, :]) - update
        for hook in hooks.get(nxt, ()):
            hook()


def per_device_kernel(
    table_ref, select_ref, keep_ref, ids_ref, place_ref, panels_out, schur_out,
    w_ref, x_refs, panels_ref, schur_ref, cols_right_ref, col_thirds, row_thirds, col_panel, row_panel, sems,
):
    n_rows, n_piv = panels_ref.shape
    cols_n = schur_ref.shape[1]
    chunk = row_thirds.shape[1]
    row_start = lax.axis_index("row") * n_rows
    col_start = lax.axis_index("col") * cols_n
    half = n_piv // 2
    place = place_ref[...]
    left, right, norm = features_of(select_ref[...], split3(table_ref[...]), keep_ref[...], place)
    own = iota((n_piv, n_piv), 0) == iota((n_piv, n_piv), 1)
    w_ref[...] = rbf(left, norm, right) + jnp.where(own, 0.1, 0.0)

    def run_features(start, count):
        rows = count // PER_ROW
        table = split3(table_ref[pl.ds(pl.multiple_of(start // PER_ROW, SUB), rows), :])
        select = (iota((count, rows), 0) // PER_ROW == iota((count, rows), 1)).astype(BF16)
        keep = (iota((count, LANES), 0) % PER_ROW == iota((count, LANES), 1) // DIM).astype(F32)
        return features_of(select, table, keep, place)

    def columns(out, at, start, count, side, norm):
        ids = start + iota((count, n_piv), 0)
        c = rbf(side, norm, right) + jnp.where(ids == ids_ref[:1, :], 0.1, 0.0)
        for i, part in enumerate(split3(c)):
            out[i, at : at + count, :] = part

    def col_columns():
        side, cols_right, norm = run_features(col_start, cols_n)
        cols_right_ref[...] = cols_right
        columns(col_thirds, 0, col_start, cols_n, side, norm)

    def row_columns(at, part, count):
        start = row_start + at + part
        side, _, norm = run_features(start, count)
        columns(row_thirds, part, start, count, side, norm)
        ids_row = start + iota((count, cols_n), 0)
        ids_col = col_start + iota((count, cols_n), 1)
        schur_ref[pl.ds(at + part, count), :] = rbf(side, norm, cols_right_ref[...]) + jnp.where(ids_row == ids_col, 0.1, 0.0)

    def panel_half(c_thirds, k):
        upto = (k + 1) * half
        return dot6([c_thirds[i, :, :upto] for i in range(3)], [x[k * half : upto, :upto] for x in x_refs])

    def col_half(k):
        for i, part in enumerate(split3(panel_half(col_thirds, k))):
            col_panel[i, :, k * half : (k + 1) * half] = part

    def row_half(at, k):
        panel = panel_half(row_thirds, k)
        panels_ref[pl.ds(at, chunk), k * half : (k + 1) * half] = panel
        for i, part in enumerate(split3(panel)):
            row_panel[i, :, k * half : (k + 1) * half] = part

    def schur_half(at, k):
        here = slice(k * half, (k + 1) * half)
        low = dot6([row_panel[i, :, here] for i in range(3)], [col_panel[i, :, here] for i in range(3)])
        schur_ref[pl.ds(at, chunk), :] = schur_ref[pl.ds(at, chunk), :] - low

    panel_copies = [
        pltpu.make_async_copy(
            panels_ref.at[:, k * half : (k + 1) * half], panels_out.at[:, k * half : (k + 1) * half], sems.at[k]
        )
        for k in range(2)
    ]
    schur_copy = pltpu.make_async_copy(schur_ref, schur_out, sems.at[2])
    if n_rows == chunk:
        q = chunk // 2
        hooks = {
            2 * BLOCK: [col_columns],
            4 * BLOCK: [lambda: row_columns(0, 0, q)],
            6 * BLOCK: [lambda: row_columns(0, q, q)],
            9 * BLOCK: [lambda: row_half(0, 0), panel_copies[0].start],
            11 * BLOCK: [lambda: col_half(0)],
            13 * BLOCK: [lambda: schur_half(0, 0)],
        }
        inverse_factor(w_ref, x_refs, n_piv, hooks)
        row_half(0, 1)
        panel_copies[1].start()
        col_half(1)
        schur_half(0, 1)
        schur_copy.start()
    else:
        inverse_factor(w_ref, x_refs, n_piv, {})
        col_columns()
        col_half(0)
        col_half(1)

        @pl.loop(0, n_rows // chunk)
        def _(i):
            at = pl.multiple_of(i * chunk, chunk)
            row_columns(at, 0, chunk)
            for k in range(2):
                row_half(at, k)
                schur_half(at, k)

        for copy in panel_copies:
            copy.start()
        schur_copy.start()
    for copy in panel_copies:
        copy.wait()
    schur_copy.wait()


def per_device(points, pivots_first, pivots_second):
    per_dev = points.shape[1]
    n_row = lax.axis_size("row")
    n_col = lax.axis_size("col")
    rows_n = per_dev * n_col
    cols_n = per_dev * n_row
    n_piv = pivots_first.shape[0] + pivots_second.shape[0]
    n_tab = n_row * n_col * per_dev * DIM // LANES
    vmem = pl.BlockSpec(memory_space=pltpu.VMEM)
    params = pltpu.CompilerParams(vmem_limit_bytes=VMEM_BYTES)
    copies, *found = pl.pallas_call(
        pack_kernel,
        out_shape=(
            jax.ShapeDtypeStruct((n_tab, LANES), F32),
            jax.ShapeDtypeStruct((n_piv, n_tab), BF16),
            jax.ShapeDtypeStruct((n_piv, LANES), F32),
            jax.ShapeDtypeStruct((SUB, n_piv), jnp.int32),
            jax.ShapeDtypeStruct((3 * LANES, 3 * LANES), BF16),
        ),
        in_specs=[pl.BlockSpec(memory_space=pltpu.HBM)] * 3,
        out_specs=(vmem,) * 5,
        scratch_shapes=[
            pltpu.VMEM((DIM, per_dev), F32),
            pltpu.VMEM((1, pivots_first.shape[0]), jnp.int32),
            pltpu.VMEM((1, pivots_second.shape[0]), jnp.int32),
            pltpu.SemaphoreType.DMA((3,)),
        ],
        compiler_params=params,
        name="pack",
    )(*(pltpu.with_memory_space_constraint(x, pltpu.HBM) for x in (points, pivots_first[None, :], pivots_second[None, :])))
    table = lax.all_to_all(copies, ("row", "col"), 0, 0, tiled=True)
    table, *found = lax.optimization_barrier((table, *found))
    chunk = min(rows_n, 256)
    return pl.pallas_call(
        per_device_kernel,
        out_shape=(jax.ShapeDtypeStruct((rows_n, n_piv), F32), jax.ShapeDtypeStruct((rows_n, cols_n), F32)),
        in_specs=[vmem] * 5,
        out_specs=(pl.BlockSpec(memory_space=pl.ANY),) * 2,
        scratch_shapes=[
            pltpu.VMEM((n_piv, n_piv), F32),
            [pltpu.VMEM((n_piv, n_piv), BF16)] * 3,
            pltpu.VMEM((rows_n, n_piv), F32),
            pltpu.VMEM((rows_n, cols_n), F32),
            pltpu.VMEM((cols_n, LANES), BF16),
            pltpu.VMEM((3, cols_n, n_piv), BF16),
            pltpu.VMEM((3, chunk, n_piv), BF16),
            pltpu.VMEM((3, cols_n, n_piv), BF16),
            pltpu.VMEM((3, chunk, n_piv), BF16),
            pltpu.SemaphoreType.DMA((3,)),
        ],
        compiler_params=params,
        name="pivoted_cholesky",
    )(table, *found)


def solution(mesh):
    return jax.shard_map(
        per_device,
        mesh=mesh,
        in_specs=(P(None, ("row", "col")), P(), P()),
        out_specs=(P("row", None), P("row", "col")),
        check_vma=False,
    )
```

```python
import functools

import jax
import jax.numpy as jnp
from jax import lax
from jax.experimental import pallas as pl
from jax.experimental.pallas import tpu as pltpu
from jax.sharding import PartitionSpec as P

DIM = 16
LANES = 128
SUB = 8
BLOCK = 16
PER_ROW = LANES // DIM
VMEM_BYTES = 24 * 2**20
F32 = jnp.float32
BF16 = jnp.bfloat16
NN = (((1,), (0,)), ((), ()))
NT = (((1,), (1,)), ((), ()))
TN = (((0,), (0,)), ((), ()))
LEFT = (0, 0, 1, 1, 0, 2)
RIGHT = (0, 1, 0, 1, 2, 0)
NORM = len(LEFT) * DIM


def iota(shape, axis):
    return lax.broadcasted_iota(jnp.int32, shape, axis)


def dot(a, b, dims):
    return lax.dot_general(a, b, dims, preferred_element_type=F32)


def split3(a):
    hi = a.astype(BF16)
    rest = a - hi.astype(F32)
    mid = rest.astype(BF16)
    return hi, mid, (rest - mid.astype(F32)).astype(BF16)


def dot6(a, b):
    n = b[0].shape[0]
    wide = dot(
        jnp.concatenate([a[0], a[1]], axis=1),
        jnp.concatenate([jnp.concatenate([b[0], b[0]], axis=1), jnp.concatenate([b[1], b[1]], axis=1)], axis=0),
        NT,
    )
    rest = dot(jnp.concatenate([a[0], a[2]], axis=1), jnp.concatenate([b[2], b[0]], axis=1), NT)
    return wide[:, :n] + (wide[:, n:] + rest)


def pack_kernel(points_in, first_in, second_in, table_ref, select_ref, keep_ref, ids_ref, place_ref, points_ref, first_ref, second_ref, sems):
    copies = [
        pltpu.make_async_copy(src, dst, sems.at[i])
        for i, (src, dst) in enumerate(((points_in, points_ref), (first_in, first_ref), (second_in, second_ref)))
    ]
    for copy in copies:
        copy.start()
    lane = iota((LANES, LANES), 1)
    same = lane % DIM == iota((LANES, LANES), 0) % DIM
    for third in range(3):
        for side, pattern in enumerate((LEFT, RIGHT)):
            hit = None
            for group, which in enumerate(pattern):
                if which == third:
                    here = lane // DIM == group
                    hit = here if hit is None else hit | here
            place_ref[third * LANES : (third + 1) * LANES, side * LANES : (side + 1) * LANES] = (same & hit).astype(BF16)
        place_ref[third * LANES : (third + 1) * LANES, 2 * LANES :] = (same & (lane < DIM)).astype(BF16)
    for copy in copies:
        copy.wait()
    n = points_ref.shape[1]
    spread_to = (iota((DIM, LANES), 1) % DIM == iota((DIM, LANES), 0)).astype(BF16)
    wide = None
    for part in split3(points_ref[...]):
        x = dot(part, spread_to, TN)
        wide = x if wide is None else wide + x
    wide = jnp.where(iota((n, LANES), 1) // DIM == iota((n, LANES), 0) % PER_ROW, wide, 0.0)
    block = jnp.concatenate([jnp.sum(wide[i : i + PER_ROW, :], axis=0, keepdims=True) for i in range(0, n, PER_ROW)], axis=0)
    table_ref[...] = jnp.concatenate([block] * (table_ref.shape[0] // block.shape[0]), axis=0)
    at = 0
    for ref in (first_ref, second_ref):
        count = ref.shape[1]
        ids_ref[:, at : at + count] = jnp.broadcast_to(ref[...], (SUB, count))
        ids = jnp.broadcast_to(ref[...].astype(F32), (LANES, count)).T.astype(jnp.int32)
        for t in range(0, table_ref.shape[0], LANES):
            select_ref[at : at + count, t : t + LANES] = (ids // PER_ROW == t + iota((count, LANES), 1)).astype(BF16)
        keep_ref[at : at + count, :] = (ids % PER_ROW == iota((count, LANES), 1) // DIM).astype(F32)
        at += count


def features_of(select, table, keep, place):
    n = select.shape[0]
    thirds = jnp.concatenate([(dot(select, part, NN) * keep).astype(BF16) for part in table], axis=1)
    both = dot(thirds, place, NN)
    x = both[:, 2 * LANES :]
    norm = jnp.sum(x * x, axis=1, keepdims=True)
    right = both[:, LANES : 2 * LANES]
    for i, part in enumerate(split3(jnp.broadcast_to(norm, (n, LANES)))):
        right = jnp.where(iota((n, LANES), 1) == NORM + i, part.astype(F32), right)
    return both[:, :LANES], right.astype(BF16), norm


def rbf(left, norm, right):
    n = left.shape[0]
    lane = iota((2 * SUB, LANES), 1)
    ones = ((lane >= NORM) & (lane < NORM + 3)).astype(BF16)
    lead = iota((n, LANES), 1) < DIM
    both = dot(jnp.concatenate([ones, jnp.where(lead, left, 0.0).astype(BF16), jnp.where(lead, 0.0, left).astype(BF16)], axis=0), right, NT)
    inner = both[2 * SUB : 2 * SUB + n] + both[2 * SUB + n :]
    return jnp.exp((norm + both[:1] - 2.0 * inner) * (-1.0 / DIM))


def row_of(tile, s):
    return jnp.broadcast_to(tile[s : s + 1, :], (SUB, LANES))


def spread(x):
    return jnp.broadcast_to(jnp.sum(x, axis=1, keepdims=True), (SUB, LANES))


def eliminate(rows, first_lane, more):
    sub = lax.broadcasted_iota(jnp.int32, (SUB, LANES), 0)
    lane = lax.broadcasted_iota(jnp.int32, (SUB, LANES), 1)
    at, off = first_lane // LANES, first_lane % LANES
    at2, off2 = (first_lane + BLOCK) // LANES, (first_lane + BLOCK) % LANES
    n_lt = len(rows[0])
    n_cur = BLOCK // SUB
    n_tiles = 2 * n_cur if more else n_cur
    cols = [
        [spread(jnp.where(lane == off + j, rows[i][at], 0.0)) if i >= j // SUB else None for i in range(n_cur)] for j in range(BLOCK)
    ]
    if more:
        for j in range(BLOCK):
            row = row_of(rows[j // SUB][at2], j % SUB)
            cols[j] += [spread(jnp.where(lane == off2 + i * SUB + sub, row, 0.0)) for i in range(n_cur)]
    own = (lane >= off) & (lane < off + BLOCK)
    rows = [list(r) for r in rows]
    for i in range(n_cur):
        rows[i][at] = jnp.where(own, (lane == off + i * SUB + sub).astype(F32), rows[i][at])
    if more:
        rows += [[jnp.zeros((SUB, LANES), F32) for _ in range(n_lt)] for _ in range(n_cur)]
    scaled = []
    for it in range(n_cur):
        shift = jnp.zeros((SUB, LANES), F32)
        scale = jnp.zeros((SUB, LANES), F32)
        for sl in range(0, SUB, 2):
            s = it * SUB + sl
            a = row_of(cols[s][it], sl)
            b = row_of(cols[s][it], sl + 1)
            c = row_of(cols[s + 1][it], sl + 1)
            det = a * c - b * b
            rdet = 1.0 / det
            ra = lax.rsqrt(a)
            ba = b * (ra * ra)
            rc = lax.rsqrt(c - b * ba)
            scale = jnp.where(sub == sl, ra, jnp.where(sub == sl + 1, rc, scale))
            shift = jnp.where(sub == sl + 1, ba, shift)
            begin = it if sl + 2 < SUB else it + 1
            m0, m1 = [None] * n_tiles, [None] * n_tiles
            for i in range(begin, n_tiles):
                u0, u1 = cols[s][i], cols[s + 1][i]
                m0[i] = (u0 * c - u1 * b) * rdet
                m1[i] = (u1 * a - u0 * b) * rdet
                if i == it:
                    m0[i] = jnp.where(sub > sl + 1, m0[i], 0.0)
                    m1[i] = jnp.where(sub > sl + 1, m1[i], 0.0)
            for j in range(s + 2, BLOCK):
                x0 = row_of(cols[s][j // SUB], j % SUB)
                x1 = row_of(cols[s + 1][j // SUB], j % SUB)
                for i in range(max(begin, j // SUB), n_tiles):
                    cols[j][i] = cols[j][i] - (m0[i] * x0 + m1[i] * x1)
            for t in range(n_lt):
                y0 = row_of(rows[it][t], sl)
                y1 = row_of(rows[it][t], sl + 1)
                for i in range(begin, n_tiles):
                    rows[i][t] = rows[i][t] - (m0[i] * y0 + m1[i] * y1)
        scaled.append([(r - shift * pltpu.roll(r, 1, 0)) * scale for r in rows[it]])
    return scaled, rows[n_cur:]


def inverse_factor(w_ref, x_refs, n, hooks):
    n_lt = n // LANES
    n_cur = BLOCK // SUB
    lane = iota((SUB, LANES), 1)

    def load(i, t):
        return w_ref[i * SUB : (i + 1) * SUB, t * LANES : (t + 1) * LANES]

    rows = [[load(i, t) for t in range(n_lt)] for i in range(n_cur)]
    for r in range(0, n, BLOCK):
        nxt = r + BLOCK
        at, off = r // LANES, r % LANES
        own = (lane >= off) & (lane < off + BLOCK)
        done, below = eliminate(rows, r, nxt < n)
        if nxt < n:
            rows = []
            for i in range(n_cur):
                tiles = [load(nxt // SUB + i, t) for t in range(n_lt)]
                tiles[at] = jnp.where(own, 0.0, tiles[at])
                rows.append([tile + more for tile, more in zip(tiles, below[i])])
        whole = jnp.concatenate([jnp.concatenate(t, axis=1) for t in done], axis=0)
        thirds = split3(whole)
        width = (at + 1) * LANES
        inside = iota((BLOCK, width), 1) < nxt
        for x_ref, part in zip(x_refs, thirds):
            x_ref[r:nxt, :width] = jnp.where(inside, part[:, :width].astype(F32), 0.0).astype(BF16)
        rest = nxt + BLOCK
        if rest < n:
            base = rest // LANES * LANES
            left = jnp.concatenate([thirds[i] for i in LEFT], axis=0)[:, base:].T
            right = jnp.concatenate([thirds[i] for i in RIGHT], axis=0)
            cuts = [rest, rest + BLOCK, n] if rest + BLOCK < n else [rest, n]
            for begin, end in zip(cuts, cuts[1:]):
                update = dot(left[begin - base : end - base, :], right, NN)
                wide = iota((end - begin, n), 1)
                w_ref[begin:end, :] = jnp.where((wide >= r) & (wide < nxt), 0.0, w_ref[begin:end, :]) - update
        for hook in hooks.get(nxt, ()):
            hook()


def per_device_kernel(
    table_ref, select_ref, keep_ref, ids_ref, place_ref, panels_out, schur_out,
    w_refs, x_refs, between_ref, panels_ref, schur_ref, cols_right_ref, col_thirds, row_thirds, col_second, row_second,
    col_panel, row_panel, sems,
):
    n_rows, n_piv = panels_ref.shape
    cols_n = schur_ref.shape[1]
    chunk = row_thirds.shape[1]
    row_start = lax.axis_index("row") * n_rows
    col_start = lax.axis_index("col") * cols_n
    half = n_piv // 2
    place = place_ref[...]
    left, right, norm = features_of(select_ref[...], split3(table_ref[...]), keep_ref[...], place)
    own = jnp.where(iota((half, half), 0) == iota((half, half), 1), 0.1, 0.0)
    w_refs[0][...] = rbf(left[:half], norm[:half], right[:half]) + own

    def of(ref, k):
        return [ref[i, :, k * half : (k + 1) * half] for i in range(3)]

    def keep_thirds(ref, k, value):
        for i, part in enumerate(split3(value)):
            ref[i, :, k * half : (k + 1) * half] = part

    def second_pivots():
        k = rbf(left[half:], norm[half:], right)
        keep_thirds(between_ref, 0, k[:, :half])
        w_refs[1][...] = k[:, half:] + own

    def second_block():
        between = split3(dot6(of(between_ref, 0), [x[...] for x in x_refs[:3]]))
        for i, part in enumerate(between):
            between_ref[i] = part
        w_refs[1][...] = w_refs[1][...] - dot6(between, between)

    def run_features(start, count):
        rows = count // PER_ROW
        table = split3(table_ref[pl.ds(pl.multiple_of(start // PER_ROW, SUB), rows), :])
        select = (iota((count, rows), 0) // PER_ROW == iota((count, rows), 1)).astype(BF16)
        keep = (iota((count, LANES), 0) % PER_ROW == iota((count, LANES), 1) // DIM).astype(F32)
        return features_of(select, table, keep, place)

    def columns(thirds, second, at, start, count, side, norm):
        ids = start + iota((count, n_piv), 0)
        c = rbf(side, norm, right) + jnp.where(ids == ids_ref[:1, :], 0.1, 0.0)
        for i, part in enumerate(split3(c[:, :half])):
            thirds[i, at : at + count, :half] = part
        second[at : at + count, :] = c[:, half:]

    def col_columns():
        side, cols_right, norm = run_features(col_start, cols_n)
        cols_right_ref[...] = cols_right
        columns(col_thirds, col_second, 0, col_start, cols_n, side, norm)

    def row_columns(at, part, count):
        start = row_start + at + part
        side, _, norm = run_features(start, count)
        columns(row_thirds, row_second, part, start, count, side, norm)
        ids_row = start + iota((count, cols_n), 0)
        ids_col = col_start + iota((count, cols_n), 1)
        schur_ref[pl.ds(at + part, count), :] = rbf(side, norm, cols_right_ref[...]) + jnp.where(ids_row == ids_col, 0.1, 0.0)

    def col_half(k):
        keep_thirds(col_panel, k, dot6(of(col_thirds, k), [x[...] for x in x_refs[3 * k : 3 * k + 3]]))

    def row_half(at, k):
        panel = dot6(of(row_thirds, k), [x[...] for x in x_refs[3 * k : 3 * k + 3]])
        panels_ref[pl.ds(at, chunk), k * half : (k + 1) * half] = panel
        keep_thirds(row_panel, k, panel)

    def second_columns(thirds, second, panel):
        between = [between_ref[i] for i in range(3)]
        keep_thirds(thirds, 1, second[...] - dot6(of(panel, 0), between))

    def schur_half(at, k):
        schur_ref[pl.ds(at, chunk), :] = schur_ref[pl.ds(at, chunk), :] - dot6(of(row_panel, k), of(col_panel, k))

    panel_copies = [
        pltpu.make_async_copy(
            panels_ref.at[:, k * half : (k + 1) * half], panels_out.at[:, k * half : (k + 1) * half], sems.at[k]
        )
        for k in range(2)
    ]
    schur_copy = pltpu.make_async_copy(schur_ref, schur_out, sems.at[2])
    if n_rows == chunk:
        q = chunk // 2
        first = {2 * BLOCK: [second_pivots], 4 * BLOCK: [col_columns]}
        inverse_factor(w_refs[0], x_refs[:3], half, first)
        second_block()
        row_columns(0, 0, chunk)
        second = {1 * BLOCK: [lambda: row_half(0, 0), panel_copies[0].start], 2 * BLOCK: [lambda: col_half(0)], 3 * BLOCK: [lambda: second_columns(row_thirds, row_second, row_panel)], 5 * BLOCK: [lambda: second_columns(col_thirds, col_second, col_panel)], 6 * BLOCK: [lambda: schur_half(0, 0)]}
        inverse_factor(w_refs[1], x_refs[3:], half, second)
        row_half(0, 1)
        panel_copies[1].start()
        col_half(1)
        schur_half(0, 1)
        schur_copy.start()
    else:
        inverse_factor(w_refs[0], x_refs[:3], half, {})
        second_pivots()
        second_block()
        inverse_factor(w_refs[1], x_refs[3:], half, {})
        col_columns()
        col_half(0)
        second_columns(col_thirds, col_second, col_panel)
        col_half(1)

        @pl.loop(0, n_rows // chunk)
        def _(i):
            at = pl.multiple_of(i * chunk, chunk)
            row_columns(at, 0, chunk)
            row_half(at, 0)
            second_columns(row_thirds, row_second, row_panel)
            row_half(at, 1)
            for k in range(2):
                schur_half(at, k)

        for copy in panel_copies:
            copy.start()
        schur_copy.start()
    for copy in panel_copies:
        copy.wait()
    schur_copy.wait()


def per_device(points, pivots_first, pivots_second):
    per_dev = points.shape[1]
    n_row = lax.axis_size("row")
    n_col = lax.axis_size("col")
    rows_n = per_dev * n_col
    cols_n = per_dev * n_row
    n_piv = pivots_first.shape[0] + pivots_second.shape[0]
    n_tab = n_row * n_col * per_dev * DIM // LANES
    vmem = pl.BlockSpec(memory_space=pltpu.VMEM)
    params = pltpu.CompilerParams(vmem_limit_bytes=VMEM_BYTES)
    copies, *found = pl.pallas_call(
        pack_kernel,
        out_shape=(
            jax.ShapeDtypeStruct((n_tab, LANES), F32),
            jax.ShapeDtypeStruct((n_piv, n_tab), BF16),
            jax.ShapeDtypeStruct((n_piv, LANES), F32),
            jax.ShapeDtypeStruct((SUB, n_piv), jnp.int32),
            jax.ShapeDtypeStruct((3 * LANES, 3 * LANES), BF16),
        ),
        in_specs=[pl.BlockSpec(memory_space=pltpu.HBM)] * 3,
        out_specs=(vmem,) * 5,
        scratch_shapes=[
            pltpu.VMEM((DIM, per_dev), F32),
            pltpu.VMEM((1, pivots_first.shape[0]), jnp.int32),
            pltpu.VMEM((1, pivots_second.shape[0]), jnp.int32),
            pltpu.SemaphoreType.DMA((3,)),
        ],
        compiler_params=params,
        name="pack",
    )(*(pltpu.with_memory_space_constraint(x, pltpu.HBM) for x in (points, pivots_first[None, :], pivots_second[None, :])))
    table = lax.all_to_all(copies, ("row", "col"), 0, 0, tiled=True)
    table, *found = lax.optimization_barrier((table, *found))
    chunk = min(rows_n, 256)
    half = n_piv // 2
    return pl.pallas_call(
        per_device_kernel,
        out_shape=(jax.ShapeDtypeStruct((rows_n, n_piv), F32), jax.ShapeDtypeStruct((rows_n, cols_n), F32)),
        in_specs=[vmem] * 5,
        out_specs=(pl.BlockSpec(memory_space=pl.ANY),) * 2,
        scratch_shapes=[
            [pltpu.VMEM((half, half), F32)] * 2,
            [pltpu.VMEM((half, half), BF16)] * 6,
            pltpu.VMEM((3, half, half), BF16),
            pltpu.VMEM((rows_n, n_piv), F32),
            pltpu.VMEM((rows_n, cols_n), F32),
            pltpu.VMEM((cols_n, LANES), BF16),
            pltpu.VMEM((3, cols_n, n_piv), BF16),
            pltpu.VMEM((3, chunk, n_piv), BF16),
            pltpu.VMEM((cols_n, half), F32),
            pltpu.VMEM((chunk, half), F32),
            pltpu.VMEM((3, cols_n, n_piv), BF16),
            pltpu.VMEM((3, chunk, n_piv), BF16),
            pltpu.SemaphoreType.DMA((3,)),
        ],
        compiler_params=params,
        name="pivoted_cholesky",
    )(table, *found)


def solution(mesh):
    return jax.shard_map(
        per_device,
        mesh=mesh,
        in_specs=(P(None, ("row", "col")), P(), P()),
        out_specs=(P("row", None), P("row", "col")),
        check_vma=False,
    )
```

```python
import functools

import jax
import jax.numpy as jnp
from jax import lax
from jax.experimental import pallas as pl
from jax.experimental.pallas import tpu as pltpu
from jax.sharding import PartitionSpec as P

DIM = 16
LANES = 128
SUB = 8
BLOCK = 16
PER_ROW = LANES // DIM
VMEM_BYTES = 24 * 2**20
F32 = jnp.float32
BF16 = jnp.bfloat16
NN = (((1,), (0,)), ((), ()))
NT = (((1,), (1,)), ((), ()))
TN = (((0,), (0,)), ((), ()))
LEFT = (0, 0, 1, 1, 0, 2)
RIGHT = (0, 1, 0, 1, 2, 0)
NORM = len(LEFT) * DIM


def iota(shape, axis):
    return lax.broadcasted_iota(jnp.int32, shape, axis)


def dot(a, b, dims):
    return lax.dot_general(a, b, dims, preferred_element_type=F32)


def split3(a):
    hi = a.astype(BF16)
    rest = a - hi.astype(F32)
    mid = rest.astype(BF16)
    return hi, mid, (rest - mid.astype(F32)).astype(BF16)


def dot6(a, b):
    n = b[0].shape[0]
    wide = dot(
        jnp.concatenate([a[0], a[1]], axis=1),
        jnp.concatenate([jnp.concatenate([b[0], b[0]], axis=1), jnp.concatenate([b[1], b[1]], axis=1)], axis=0),
        NT,
    )
    rest = dot(jnp.concatenate([a[0], a[2]], axis=1), jnp.concatenate([b[2], b[0]], axis=1), NT)
    return wide[:, :n] + (wide[:, n:] + rest)


def pack_kernel(points_in, first_in, second_in, table_ref, select_ref, keep_ref, ids_ref, place_ref, points_ref, first_ref, second_ref, sems):
    copies = [
        pltpu.make_async_copy(src, dst, sems.at[i])
        for i, (src, dst) in enumerate(((points_in, points_ref), (first_in, first_ref), (second_in, second_ref)))
    ]
    for copy in copies:
        copy.start()
    lane = iota((LANES, LANES), 1)
    same = lane % DIM == iota((LANES, LANES), 0) % DIM
    for third in range(3):
        for side, pattern in enumerate((LEFT, RIGHT)):
            hit = None
            for group, which in enumerate(pattern):
                if which == third:
                    here = lane // DIM == group
                    hit = here if hit is None else hit | here
            place_ref[third * LANES : (third + 1) * LANES, side * LANES : (side + 1) * LANES] = (same & hit).astype(BF16)
        place_ref[third * LANES : (third + 1) * LANES, 2 * LANES :] = (same & (lane < DIM)).astype(BF16)
    for copy in copies:
        copy.wait()
    n = points_ref.shape[1]
    tall = jnp.concatenate([points_ref[...], jnp.zeros((DIM, LANES - n), F32)], axis=1)
    tall = jnp.concatenate([tall, jnp.zeros((LANES - DIM, LANES), F32)], axis=0).T
    block = []
    for i in range(0, n, PER_ROW):
        moved = pltpu.roll(tall[i : i + PER_ROW, :], 0, 1, stride=DIM, stride_axis=0)
        block.append(jnp.sum(moved, axis=0, keepdims=True))
    block = jnp.concatenate(block, axis=0)
    table_ref[...] = jnp.concatenate([block] * (table_ref.shape[0] // block.shape[0]), axis=0)
    at = 0
    for ref in (first_ref, second_ref):
        count = ref.shape[1]
        ids_ref[:, at : at + count] = jnp.broadcast_to(ref[...], (SUB, count))
        ids = jnp.broadcast_to(ref[...].astype(F32), (LANES, count)).T.astype(jnp.int32)
        for t in range(0, table_ref.shape[0], LANES):
            select_ref[at : at + count, t : t + LANES] = (ids // PER_ROW == t + iota((count, LANES), 1)).astype(BF16)
        keep_ref[at : at + count, :] = (ids % PER_ROW == iota((count, LANES), 1) // DIM).astype(F32)
        at += count


def features_of(select, table, keep, place):
    n = select.shape[0]
    thirds = jnp.concatenate([(dot(select, part, NN) * keep).astype(BF16) for part in table], axis=1)
    both = dot(thirds, place, NN)
    x = both[:, 2 * LANES :]
    norm = jnp.sum(x * x, axis=1, keepdims=True)
    right = both[:, LANES : 2 * LANES]
    for i, part in enumerate(split3(jnp.broadcast_to(norm, (n, LANES)))):
        right = jnp.where(iota((n, LANES), 1) == NORM + i, part.astype(F32), right)
    return both[:, :LANES], right.astype(BF16), norm


def rbf(left, norm, right):
    n = left.shape[0]
    lane = iota((2 * SUB, LANES), 1)
    ones = ((lane >= NORM) & (lane < NORM + 3)).astype(BF16)
    lead = iota((n, LANES), 1) < DIM
    both = dot(jnp.concatenate([ones, jnp.where(lead, left, 0.0).astype(BF16), jnp.where(lead, 0.0, left).astype(BF16)], axis=0), right, NT)
    inner = both[2 * SUB : 2 * SUB + n] + both[2 * SUB + n :]
    return jnp.exp((norm + both[:1] - 2.0 * inner) * (-1.0 / DIM))


def row_of(tile, s):
    return jnp.broadcast_to(tile[s : s + 1, :], (SUB, LANES))


def spread(x):
    return jnp.broadcast_to(jnp.sum(x, axis=1, keepdims=True), (SUB, LANES))


def eliminate(rows, first_lane, more):
    sub = lax.broadcasted_iota(jnp.int32, (SUB, LANES), 0)
    lane = lax.broadcasted_iota(jnp.int32, (SUB, LANES), 1)
    at, off = first_lane // LANES, first_lane % LANES
    at2, off2 = (first_lane + BLOCK) // LANES, (first_lane + BLOCK) % LANES
    n_lt = len(rows[0])
    n_cur = BLOCK // SUB
    n_tiles = 2 * n_cur if more else n_cur
    cols = [
        [spread(jnp.where(lane == off + j, rows[i][at], 0.0)) if i >= j // SUB else None for i in range(n_cur)] for j in range(BLOCK)
    ]

    def add_below(it):
        for j in range(it * SUB, (it + 1) * SUB):
            row = row_of(rows[it][at2], j % SUB)
            cols[j] += [spread(jnp.where(lane == off2 + i * SUB + sub, row, 0.0)) for i in range(n_cur)]

    if more:
        add_below(0)
    rows = [list(r) for r in rows]
    if more:
        rows += [[jnp.zeros((SUB, LANES), F32) for _ in range(n_lt)] for _ in range(n_cur)]
    scaled = []
    for it in range(n_cur):
        if more and it > 0:
            add_below(it)
        own = (lane >= off + it * SUB) & (lane < off + (it + 1) * SUB)
        for i in range(it, n_tiles):
            unit = (lane == off + i * SUB + sub).astype(F32) if i == it else jnp.zeros((SUB, LANES), F32)
            rows[i][at] = jnp.where(own, unit, rows[i][at])
        shift = jnp.zeros((SUB, LANES), F32)
        scale = jnp.zeros((SUB, LANES), F32)
        for sl in range(0, SUB, 2):
            s = it * SUB + sl
            a = row_of(cols[s][it], sl)
            b = row_of(cols[s][it], sl + 1)
            c = row_of(cols[s + 1][it], sl + 1)
            det = a * c - b * b
            rdet = 1.0 / det
            ra = lax.rsqrt(a)
            ba = b * (ra * ra)
            rc = lax.rsqrt(c - b * ba)
            scale = jnp.where(sub == sl, ra, jnp.where(sub == sl + 1, rc, scale))
            shift = jnp.where(sub == sl + 1, ba, shift)
            begin = it if sl + 2 < SUB else it + 1
            m0, m1 = [None] * n_tiles, [None] * n_tiles
            for i in range(begin, n_tiles):
                u0, u1 = cols[s][i], cols[s + 1][i]
                m0[i] = (u0 * c - u1 * b) * rdet
                m1[i] = (u1 * a - u0 * b) * rdet
                if i == it:
                    m0[i] = jnp.where(sub > sl + 1, m0[i], 0.0)
                    m1[i] = jnp.where(sub > sl + 1, m1[i], 0.0)
            for j in range(s + 2, BLOCK):
                x0 = row_of(cols[s][j // SUB], j % SUB)
                x1 = row_of(cols[s + 1][j // SUB], j % SUB)
                for i in range(max(begin, j // SUB), len(cols[j])):
                    cols[j][i] = cols[j][i] - (m0[i] * x0 + m1[i] * x1)
            for t in range(n_lt):
                y0 = row_of(rows[it][t], sl)
                y1 = row_of(rows[it][t], sl + 1)
                for i in range(begin, n_tiles):
                    rows[i][t] = rows[i][t] - (m0[i] * y0 + m1[i] * y1)
        scaled.append([(r - shift * pltpu.roll(r, 1, 0)) * scale for r in rows[it]])
        later = (lane >= off + (it + 1) * SUB) & (lane < off + BLOCK)
        if it + 1 < n_cur:
            scaled[it][at] = jnp.where(later, 0.0, scaled[it][at])
    return scaled, rows[n_cur:]


def inverse_factor(w_ref, x_refs, n, hooks):
    n_lt = n // LANES
    n_cur = BLOCK // SUB
    lane = iota((SUB, LANES), 1)

    def load(i, t):
        return w_ref[i * SUB : (i + 1) * SUB, t * LANES : (t + 1) * LANES]

    rows = [[load(i, t) for t in range(n_lt)] for i in range(n_cur)]
    for r in range(0, n, BLOCK):
        nxt = r + BLOCK
        at, off = r // LANES, r % LANES
        own = (lane >= off) & (lane < off + BLOCK)
        done, below = eliminate(rows, r, nxt < n)
        if nxt < n:
            rows = []
            for i in range(n_cur):
                tiles = [load(nxt // SUB + i, t) for t in range(n_lt)]
                tiles[at] = jnp.where(own, 0.0, tiles[at])
                rows.append([tile + more for tile, more in zip(tiles, below[i])])
        whole = jnp.concatenate([jnp.concatenate(t, axis=1) for t in done], axis=0)
        thirds = split3(whole)
        width = (at + 1) * LANES
        inside = iota((BLOCK, width), 1) < nxt
        for x_ref, part in zip(x_refs, thirds):
            x_ref[r:nxt, :width] = jnp.where(inside, part[:, :width].astype(F32), 0.0).astype(BF16)
        rest = nxt + BLOCK
        if rest < n:
            base = rest // LANES * LANES
            left = jnp.concatenate([thirds[i] for i in LEFT], axis=0)[:, base:].T
            right = jnp.concatenate([thirds[i] for i in RIGHT], axis=0)
            cuts = [rest, rest + BLOCK, n] if rest + BLOCK < n else [rest, n]
            for begin, end in zip(cuts, cuts[1:]):
                update = dot(left[begin - base : end - base, :], right, NN)
                wide = iota((end - begin, n), 1)
                w_ref[begin:end, :] = jnp.where((wide >= r) & (wide < nxt), 0.0, w_ref[begin:end, :]) - update
        for hook in hooks.get(nxt, ()):
            hook()


def per_device_kernel(
    table_ref, select_ref, keep_ref, ids_ref, place_ref, panels_out, schur_out,
    w_refs, x_refs, between_ref, panels_ref, schur_ref, cols_right_ref, col_thirds, row_thirds, col_second, row_second,
    col_panel, row_panel, sems,
):
    n_rows, n_piv = panels_ref.shape
    cols_n = schur_ref.shape[1]
    chunk = row_thirds.shape[1]
    row_start = lax.axis_index("row") * n_rows
    col_start = lax.axis_index("col") * cols_n
    half = n_piv // 2
    place = place_ref[...]
    left, right, norm = features_of(select_ref[...], split3(table_ref[...]), keep_ref[...], place)
    own = jnp.where(iota((half, half), 0) == iota((half, half), 1), 0.1, 0.0)
    w_refs[0][...] = rbf(left[:half], norm[:half], right[:half]) + own

    def of(ref, k):
        return [ref[i, :, k * half : (k + 1) * half] for i in range(3)]

    def keep_thirds(ref, k, value):
        for i, part in enumerate(split3(value)):
            ref[i, :, k * half : (k + 1) * half] = part

    def second_pivots():
        k = rbf(left[half:], norm[half:], right)
        keep_thirds(between_ref, 0, k[:, :half])
        w_refs[1][...] = k[:, half:] + own

    def second_block():
        between = split3(dot6(of(between_ref, 0), [x[...] for x in x_refs[:3]]))
        for i, part in enumerate(between):
            between_ref[i] = part
        w_refs[1][...] = w_refs[1][...] - dot6(between, between)

    def run_features(start, count):
        rows = count // PER_ROW
        table = split3(table_ref[pl.ds(pl.multiple_of(start // PER_ROW, SUB), rows), :])
        select = (iota((count, rows), 0) // PER_ROW == iota((count, rows), 1)).astype(BF16)
        keep = (iota((count, LANES), 0) % PER_ROW == iota((count, LANES), 1) // DIM).astype(F32)
        return features_of(select, table, keep, place)

    def columns(thirds, second, at, start, count, side, norm):
        ids = start + iota((count, n_piv), 0)
        c = rbf(side, norm, right) + jnp.where(ids == ids_ref[:1, :], 0.1, 0.0)
        for i, part in enumerate(split3(c[:, :half])):
            thirds[i, at : at + count, :half] = part
        second[at : at + count, :] = c[:, half:]

    def col_columns():
        side, cols_right, norm = run_features(col_start, cols_n)
        cols_right_ref[...] = cols_right
        columns(col_thirds, col_second, 0, col_start, cols_n, side, norm)

    def row_columns(at, part, count):
        start = row_start + at + part
        side, _, norm = run_features(start, count)
        columns(row_thirds, row_second, part, start, count, side, norm)
        ids_row = start + iota((count, cols_n), 0)
        ids_col = col_start + iota((count, cols_n), 1)
        schur_ref[pl.ds(at + part, count), :] = rbf(side, norm, cols_right_ref[...]) + jnp.where(ids_row == ids_col, 0.1, 0.0)

    def col_half(k):
        keep_thirds(col_panel, k, dot6(of(col_thirds, k), [x[...] for x in x_refs[3 * k : 3 * k + 3]]))

    def row_half(at, k):
        panel = dot6(of(row_thirds, k), [x[...] for x in x_refs[3 * k : 3 * k + 3]])
        panels_ref[pl.ds(at, chunk), k * half : (k + 1) * half] = panel
        keep_thirds(row_panel, k, panel)

    def second_columns(thirds, second, panel):
        between = [between_ref[i] for i in range(3)]
        keep_thirds(thirds, 1, second[...] - dot6(of(panel, 0), between))

    def schur_half(at, k):
        schur_ref[pl.ds(at, chunk), :] = schur_ref[pl.ds(at, chunk), :] - dot6(of(row_panel, k), of(col_panel, k))

    panel_copies = [
        pltpu.make_async_copy(
            panels_ref.at[:, k * half : (k + 1) * half], panels_out.at[:, k * half : (k + 1) * half], sems.at[k]
        )
        for k in range(2)
    ]
    schur_copy = pltpu.make_async_copy(schur_ref, schur_out, sems.at[2])
    if n_rows == chunk:
        q = chunk // 2
        first = {2 * BLOCK: [second_pivots], 4 * BLOCK: [col_columns]}
        inverse_factor(w_refs[0], x_refs[:3], half, first)
        second_block()
        row_columns(0, 0, chunk)
        second = {1 * BLOCK: [lambda: row_half(0, 0), panel_copies[0].start], 2 * BLOCK: [lambda: col_half(0)], 3 * BLOCK: [lambda: second_columns(row_thirds, row_second, row_panel)], 5 * BLOCK: [lambda: second_columns(col_thirds, col_second, col_panel)], 6 * BLOCK: [lambda: schur_half(0, 0)]}
        inverse_factor(w_refs[1], x_refs[3:], half, second)
        last = [jnp.concatenate([r, c], axis=0) for r, c in zip(of(row_thirds, 1), of(col_thirds, 1))]
        both = dot6(last, [x[...] for x in x_refs[3:]])
        panels_ref[:, half:] = both[:chunk]
        panel_copies[1].start()
        both = split3(both)
        schur_ref[...] = schur_ref[...] - dot6([p[:chunk] for p in both], [p[chunk:] for p in both])
        schur_copy.start()
    else:
        inverse_factor(w_refs[0], x_refs[:3], half, {})
        second_pivots()
        second_block()
        inverse_factor(w_refs[1], x_refs[3:], half, {})
        col_columns()
        col_half(0)
        second_columns(col_thirds, col_second, col_panel)
        col_half(1)

        @pl.loop(0, n_rows // chunk)
        def _(i):
            at = pl.multiple_of(i * chunk, chunk)
            row_columns(at, 0, chunk)
            row_half(at, 0)
            second_columns(row_thirds, row_second, row_panel)
            row_half(at, 1)
            for k in range(2):
                schur_half(at, k)

        for copy in panel_copies:
            copy.start()
        schur_copy.start()
    for copy in panel_copies:
        copy.wait()
    schur_copy.wait()


def per_device(points, pivots_first, pivots_second):
    per_dev = points.shape[1]
    n_row = lax.axis_size("row")
    n_col = lax.axis_size("col")
    rows_n = per_dev * n_col
    cols_n = per_dev * n_row
    n_piv = pivots_first.shape[0] + pivots_second.shape[0]
    n_tab = n_row * n_col * per_dev * DIM // LANES
    vmem = pl.BlockSpec(memory_space=pltpu.VMEM)
    params = pltpu.CompilerParams(vmem_limit_bytes=VMEM_BYTES)
    copies, *found = pl.pallas_call(
        pack_kernel,
        out_shape=(
            jax.ShapeDtypeStruct((n_tab, LANES), F32),
            jax.ShapeDtypeStruct((n_piv, n_tab), BF16),
            jax.ShapeDtypeStruct((n_piv, LANES), F32),
            jax.ShapeDtypeStruct((SUB, n_piv), jnp.int32),
            jax.ShapeDtypeStruct((3 * LANES, 3 * LANES), BF16),
        ),
        in_specs=[pl.BlockSpec(memory_space=pltpu.HBM)] * 3,
        out_specs=(vmem,) * 5,
        scratch_shapes=[
            pltpu.VMEM((DIM, per_dev), F32),
            pltpu.VMEM((1, pivots_first.shape[0]), jnp.int32),
            pltpu.VMEM((1, pivots_second.shape[0]), jnp.int32),
            pltpu.SemaphoreType.DMA((3,)),
        ],
        compiler_params=params,
        name="pack",
    )(*(pltpu.with_memory_space_constraint(x, pltpu.HBM) for x in (points, pivots_first[None, :], pivots_second[None, :])))
    table = lax.all_to_all(copies, ("row", "col"), 0, 0, tiled=True)
    table, *found = lax.optimization_barrier((table, *found))
    chunk = min(rows_n, 256)
    half = n_piv // 2
    return pl.pallas_call(
        per_device_kernel,
        out_shape=(jax.ShapeDtypeStruct((rows_n, n_piv), F32), jax.ShapeDtypeStruct((rows_n, cols_n), F32)),
        in_specs=[vmem] * 5,
        out_specs=(pl.BlockSpec(memory_space=pl.ANY),) * 2,
        scratch_shapes=[
            [pltpu.VMEM((half, half), F32)] * 2,
            [pltpu.VMEM((half, half), BF16)] * 6,
            pltpu.VMEM((3, half, half), BF16),
            pltpu.VMEM((rows_n, n_piv), F32),
            pltpu.VMEM((rows_n, cols_n), F32),
            pltpu.VMEM((cols_n, LANES), BF16),
            pltpu.VMEM((3, cols_n, n_piv), BF16),
            pltpu.VMEM((3, chunk, n_piv), BF16),
            pltpu.VMEM((cols_n, half), F32),
            pltpu.VMEM((chunk, half), F32),
            pltpu.VMEM((3, cols_n, n_piv), BF16),
            pltpu.VMEM((3, chunk, n_piv), BF16),
            pltpu.SemaphoreType.DMA((3,)),
        ],
        compiler_params=params,
        name="pivoted_cholesky",
    )(table, *found)


def solution(mesh):
    return jax.shard_map(
        per_device,
        mesh=mesh,
        in_specs=(P(None, ("row", "col")), P(), P()),
        out_specs=(P("row", None), P("row", "col")),
        check_vma=False,
    )
```

```python
import functools

import jax
import jax.numpy as jnp
from jax import lax
from jax.experimental import pallas as pl
from jax.experimental.pallas import tpu as pltpu
from jax.sharding import PartitionSpec as P

DIM = 16
LANES = 128
SUB = 8
BLOCK = 16
PER_ROW = LANES // DIM
VMEM_BYTES = 24 * 2**20
F32 = jnp.float32
BF16 = jnp.bfloat16
NN = (((1,), (0,)), ((), ()))
NT = (((1,), (1,)), ((), ()))
TN = (((0,), (0,)), ((), ()))
LEFT = (0, 0, 1, 1, 0, 2)
RIGHT = (0, 1, 0, 1, 2, 0)
NORM = len(LEFT) * DIM


def iota(shape, axis):
    return lax.broadcasted_iota(jnp.int32, shape, axis)


def dot(a, b, dims):
    return lax.dot_general(a, b, dims, preferred_element_type=F32)


def split3(a):
    hi = a.astype(BF16)
    rest = a - hi.astype(F32)
    mid = rest.astype(BF16)
    return hi, mid, (rest - mid.astype(F32)).astype(BF16)


def dot6(a, b):
    n = b[0].shape[0]
    wide = dot(
        jnp.concatenate([a[0], a[1]], axis=1),
        jnp.concatenate([jnp.concatenate([b[0], b[0]], axis=1), jnp.concatenate([b[1], b[1]], axis=1)], axis=0),
        NT,
    )
    rest = dot(jnp.concatenate([a[0], a[2]], axis=1), jnp.concatenate([b[2], b[0]], axis=1), NT)
    return wide[:, :n] + (wide[:, n:] + rest)


def pack_kernel(points_in, first_in, second_in, table_ref, select_ref, keep_ref, ids_ref, place_ref, points_ref, first_ref, second_ref, sems):
    copies = [
        pltpu.make_async_copy(src, dst, sems.at[i])
        for i, (src, dst) in enumerate(((points_in, points_ref), (first_in, first_ref), (second_in, second_ref)))
    ]
    for copy in copies:
        copy.start()
    lane = iota((LANES, LANES), 1)
    same = lane % DIM == iota((LANES, LANES), 0) % DIM
    for third in range(3):
        for side, pattern in enumerate((LEFT, RIGHT)):
            hit = None
            for group, which in enumerate(pattern):
                if which == third:
                    here = lane // DIM == group
                    hit = here if hit is None else hit | here
            place_ref[third * LANES : (third + 1) * LANES, side * LANES : (side + 1) * LANES] = (same & hit).astype(BF16)
        place_ref[third * LANES : (third + 1) * LANES, 2 * LANES :] = (same & (lane < DIM)).astype(BF16)
    for copy in copies:
        copy.wait()
    n = points_ref.shape[1]
    tall = jnp.concatenate([points_ref[...], jnp.zeros((DIM, LANES - n), F32)], axis=1)
    tall = jnp.concatenate([tall, jnp.zeros((LANES - DIM, LANES), F32)], axis=0).T
    block = []
    for i in range(0, n, PER_ROW):
        moved = pltpu.roll(tall[i : i + PER_ROW, :], 0, 1, stride=DIM, stride_axis=0)
        block.append(jnp.sum(moved, axis=0, keepdims=True))
    block = jnp.concatenate(block, axis=0)
    table_ref[...] = jnp.concatenate([block] * (table_ref.shape[0] // block.shape[0]), axis=0)
    at = 0
    for ref in (first_ref, second_ref):
        count = ref.shape[1]
        ids_ref[:, at : at + count] = jnp.broadcast_to(ref[...], (SUB, count))
        ids = jnp.broadcast_to(ref[...].astype(F32), (LANES, count)).T.astype(jnp.int32)
        for t in range(0, table_ref.shape[0], LANES):
            select_ref[at : at + count, t : t + LANES] = (ids // PER_ROW == t + iota((count, LANES), 1)).astype(BF16)
        keep_ref[at : at + count, :] = (ids % PER_ROW == iota((count, LANES), 1) // DIM).astype(F32)
        at += count


def features_of(select, table, keep, place):
    n = select.shape[0]
    thirds = jnp.concatenate([(dot(select, part, NN) * keep).astype(BF16) for part in table], axis=1)
    both = dot(thirds, place, NN)
    x = both[:, 2 * LANES :]
    norm = jnp.sum(x * x, axis=1, keepdims=True)
    right = both[:, LANES : 2 * LANES]
    for i, part in enumerate(split3(jnp.broadcast_to(norm, (n, LANES)))):
        right = jnp.where(iota((n, LANES), 1) == NORM + i, part.astype(F32), right)
    return both[:, :LANES], right.astype(BF16), norm


def rbf(left, norm, right):
    n = left.shape[0]
    lane = iota((2 * SUB, LANES), 1)
    ones = ((lane >= NORM) & (lane < NORM + 3)).astype(BF16)
    lead = iota((n, LANES), 1) < DIM
    both = dot(jnp.concatenate([ones, jnp.where(lead, left, 0.0).astype(BF16), jnp.where(lead, 0.0, left).astype(BF16)], axis=0), right, NT)
    inner = both[2 * SUB : 2 * SUB + n] + both[2 * SUB + n :]
    return jnp.exp((norm + both[:1] - 2.0 * inner) * (-1.0 / DIM))


def row_of(tile, s):
    return jnp.broadcast_to(tile[s : s + 1, :], (SUB, LANES))


def spread(x):
    return jnp.broadcast_to(jnp.sum(x, axis=1, keepdims=True), (SUB, LANES))


def eliminate(rows, first_lane, more):
    sub = lax.broadcasted_iota(jnp.int32, (SUB, LANES), 0)
    lane = lax.broadcasted_iota(jnp.int32, (SUB, LANES), 1)
    at, off = first_lane // LANES, first_lane % LANES
    at2, off2 = (first_lane + BLOCK) // LANES, (first_lane + BLOCK) % LANES
    n_lt = len(rows[0])
    n_cur = BLOCK // SUB
    n_tiles = 2 * n_cur if more else n_cur
    cols = [
        [spread(jnp.where(lane == off + j, rows[i][at], 0.0)) if i >= j // SUB else None for i in range(n_cur)] for j in range(BLOCK)
    ]

    def add_below(it):
        for j in range(it * SUB, (it + 1) * SUB):
            row = row_of(rows[it][at2], j % SUB)
            cols[j] += [spread(jnp.where(lane == off2 + i * SUB + sub, row, 0.0)) for i in range(n_cur)]

    if more:
        add_below(0)
    rows = [list(r) for r in rows]
    if more:
        rows += [[jnp.zeros((SUB, LANES), F32) for _ in range(n_lt)] for _ in range(n_cur)]
    scaled = []
    for it in range(n_cur):
        if more and it > 0:
            add_below(it)
        own = (lane >= off + it * SUB) & (lane < off + (it + 1) * SUB)
        for i in range(it, n_tiles):
            unit = (lane == off + i * SUB + sub).astype(F32) if i == it else jnp.zeros((SUB, LANES), F32)
            rows[i][at] = jnp.where(own, unit, rows[i][at])
        shift = jnp.zeros((SUB, LANES), F32)
        scale = jnp.zeros((SUB, LANES), F32)
        for sl in range(0, SUB, 2):
            s = it * SUB + sl
            a = row_of(cols[s][it], sl)
            b = row_of(cols[s][it], sl + 1)
            c = row_of(cols[s + 1][it], sl + 1)
            det = a * c - b * b
            rdet = 1.0 / det
            ra = lax.rsqrt(a)
            ba = b * (ra * ra)
            rc = lax.rsqrt(c - b * ba)
            scale = jnp.where(sub == sl, ra, jnp.where(sub == sl + 1, rc, scale))
            shift = jnp.where(sub == sl + 1, ba, shift)
            begin = it if sl + 2 < SUB else it + 1
            m0, m1 = [None] * n_tiles, [None] * n_tiles
            ar, br, cr = a * rdet, b * rdet, c * rdet
            for i in range(begin, n_tiles):
                u0, u1 = cols[s][i], cols[s + 1][i]
                if i == it:
                    m0[i] = (u0 * c - u1 * b) * rdet
                    m1[i] = (u1 * a - u0 * b) * rdet
                else:
                    m0[i] = u0 * cr - u1 * br
                    m1[i] = u1 * ar - u0 * br
                if i == it:
                    m0[i] = jnp.where(sub > sl + 1, m0[i], 0.0)
                    m1[i] = jnp.where(sub > sl + 1, m1[i], 0.0)
            for j in range(s + 2, BLOCK):
                x0 = row_of(cols[s][j // SUB], j % SUB)
                x1 = row_of(cols[s + 1][j // SUB], j % SUB)
                for i in range(max(begin, j // SUB), len(cols[j])):
                    cols[j][i] = cols[j][i] - (m0[i] * x0 + m1[i] * x1)
            for t in range(n_lt):
                y0 = row_of(rows[it][t], sl)
                y1 = row_of(rows[it][t], sl + 1)
                for i in range(begin, n_tiles):
                    rows[i][t] = rows[i][t] - (m0[i] * y0 + m1[i] * y1)
        scaled.append([(r - shift * pltpu.roll(r, 1, 0)) * scale for r in rows[it]])
        later = (lane >= off + (it + 1) * SUB) & (lane < off + BLOCK)
        if it + 1 < n_cur:
            scaled[it][at] = jnp.where(later, 0.0, scaled[it][at])
    return scaled, rows[n_cur:]


def inverse_factor(w_ref, x_refs, n, hooks):
    n_lt = n // LANES
    n_cur = BLOCK // SUB
    lane = iota((SUB, LANES), 1)

    def load(i, t):
        return w_ref[i * SUB : (i + 1) * SUB, t * LANES : (t + 1) * LANES]

    rows = [[load(i, t) for t in range(n_lt)] for i in range(n_cur)]
    for r in range(0, n, BLOCK):
        nxt = r + BLOCK
        at, off = r // LANES, r % LANES
        own = (lane >= off) & (lane < off + BLOCK)
        done, below = eliminate(rows, r, nxt < n)
        if nxt < n:
            rows = []
            for i in range(n_cur):
                tiles = [load(nxt // SUB + i, t) for t in range(n_lt)]
                tiles[at] = jnp.where(own, 0.0, tiles[at])
                rows.append([tile + more for tile, more in zip(tiles, below[i])])
        whole = jnp.concatenate([jnp.concatenate(t, axis=1) for t in done], axis=0)
        thirds = split3(whole)
        width = (at + 1) * LANES
        inside = iota((BLOCK, width), 1) < nxt
        for x_ref, part in zip(x_refs, thirds):
            x_ref[r:nxt, :width] = jnp.where(inside, part[:, :width].astype(F32), 0.0).astype(BF16)
        rest = nxt + BLOCK
        if rest < n:
            base = rest // LANES * LANES
            left = jnp.concatenate([thirds[i] for i in LEFT], axis=0)[:, base:].T
            right = jnp.concatenate([thirds[i] for i in RIGHT], axis=0)
            cuts = [rest, rest + BLOCK, n] if rest + BLOCK < n else [rest, n]
            for begin, end in zip(cuts, cuts[1:]):
                update = dot(left[begin - base : end - base, :], right, NN)
                wide = iota((end - begin, n), 1)
                w_ref[begin:end, :] = jnp.where((wide >= r) & (wide < nxt), 0.0, w_ref[begin:end, :]) - update
        for hook in hooks.get(nxt, ()):
            hook()


def per_device_kernel(
    table_ref, select_ref, keep_ref, ids_ref, place_ref, panels_out, schur_out,
    w_refs, x_refs, between_ref, panels_ref, schur_ref, cols_right_ref, col_thirds, row_thirds, col_second, row_second,
    col_panel, row_panel, sems,
):
    n_rows, n_piv = panels_ref.shape
    cols_n = schur_ref.shape[1]
    chunk = row_thirds.shape[1]
    row_start = lax.axis_index("row") * n_rows
    col_start = lax.axis_index("col") * cols_n
    half = n_piv // 2
    place = place_ref[...]
    left, right, norm = features_of(select_ref[...], split3(table_ref[...]), keep_ref[...], place)
    own = jnp.where(iota((half, half), 0) == iota((half, half), 1), 0.1, 0.0)
    w_refs[0][...] = rbf(left[:half], norm[:half], right[:half]) + own

    def of(ref, k):
        return [ref[i, :, k * half : (k + 1) * half] for i in range(3)]

    def keep_thirds(ref, k, value):
        for i, part in enumerate(split3(value)):
            ref[i, :, k * half : (k + 1) * half] = part

    def second_pivots():
        k = rbf(left[half:], norm[half:], right)
        keep_thirds(between_ref, 0, k[:, :half])
        w_refs[1][...] = k[:, half:] + own

    def second_block():
        between = split3(dot6(of(between_ref, 0), [x[...] for x in x_refs[:3]]))
        for i, part in enumerate(between):
            between_ref[i] = part
        w_refs[1][...] = w_refs[1][...] - dot6(between, between)

    def run_features(start, count):
        rows = count // PER_ROW
        table = split3(table_ref[pl.ds(pl.multiple_of(start // PER_ROW, SUB), rows), :])
        select = (iota((count, rows), 0) // PER_ROW == iota((count, rows), 1)).astype(BF16)
        keep = (iota((count, LANES), 0) % PER_ROW == iota((count, LANES), 1) // DIM).astype(F32)
        return features_of(select, table, keep, place)

    def columns(thirds, second, at, start, count, side, norm):
        ids = start + iota((count, n_piv), 0)
        c = rbf(side, norm, right) + jnp.where(ids == ids_ref[:1, :], 0.1, 0.0)
        for i, part in enumerate(split3(c[:, :half])):
            thirds[i, at : at + count, :half] = part
        second[at : at + count, :] = c[:, half:]

    def col_columns():
        side, cols_right, norm = run_features(col_start, cols_n)
        cols_right_ref[...] = cols_right
        columns(col_thirds, col_second, 0, col_start, cols_n, side, norm)

    def row_columns(at, part, count):
        start = row_start + at + part
        side, _, norm = run_features(start, count)
        columns(row_thirds, row_second, part, start, count, side, norm)
        ids_row = start + iota((count, cols_n), 0)
        ids_col = col_start + iota((count, cols_n), 1)
        schur_ref[pl.ds(at + part, count), :] = rbf(side, norm, cols_right_ref[...]) + jnp.where(ids_row == ids_col, 0.1, 0.0)

    def col_half(k):
        keep_thirds(col_panel, k, dot6(of(col_thirds, k), [x[...] for x in x_refs[3 * k : 3 * k + 3]]))

    def row_half(at, k):
        panel = dot6(of(row_thirds, k), [x[...] for x in x_refs[3 * k : 3 * k + 3]])
        panels_ref[pl.ds(at, chunk), k * half : (k + 1) * half] = panel
        keep_thirds(row_panel, k, panel)

    def second_columns(thirds, second, panel):
        between = [between_ref[i] for i in range(3)]
        keep_thirds(thirds, 1, second[...] - dot6(of(panel, 0), between))

    def schur_half(at, k):
        schur_ref[pl.ds(at, chunk), :] = schur_ref[pl.ds(at, chunk), :] - dot6(of(row_panel, k), of(col_panel, k))

    panel_copies = [
        pltpu.make_async_copy(
            panels_ref.at[:, k * half : (k + 1) * half], panels_out.at[:, k * half : (k + 1) * half], sems.at[k]
        )
        for k in range(2)
    ]
    schur_copy = pltpu.make_async_copy(schur_ref, schur_out, sems.at[2])
    if n_rows == chunk:
        q = chunk // 2
        first = {2 * BLOCK: [second_pivots], 4 * BLOCK: [col_columns]}
        inverse_factor(w_refs[0], x_refs[:3], half, first)
        second_block()
        row_columns(0, 0, chunk)
        second = {1 * BLOCK: [lambda: row_half(0, 0), panel_copies[0].start], 2 * BLOCK: [lambda: col_half(0)], 3 * BLOCK: [lambda: second_columns(row_thirds, row_second, row_panel)], 5 * BLOCK: [lambda: second_columns(col_thirds, col_second, col_panel)], 6 * BLOCK: [lambda: schur_half(0, 0)]}
        inverse_factor(w_refs[1], x_refs[3:], half, second)
        last = [jnp.concatenate([r, c], axis=0) for r, c in zip(of(row_thirds, 1), of(col_thirds, 1))]
        both = dot6(last, [x[...] for x in x_refs[3:]])
        panels_ref[:, half:] = both[:chunk]
        panel_copies[1].start()
        both = split3(both)
        schur_ref[...] = schur_ref[...] - dot6([p[:chunk] for p in both], [p[chunk:] for p in both])
        schur_copy.start()
    else:
        inverse_factor(w_refs[0], x_refs[:3], half, {})
        second_pivots()
        second_block()
        inverse_factor(w_refs[1], x_refs[3:], half, {})
        col_columns()
        col_half(0)
        second_columns(col_thirds, col_second, col_panel)
        col_half(1)

        @pl.loop(0, n_rows // chunk)
        def _(i):
            at = pl.multiple_of(i * chunk, chunk)
            row_columns(at, 0, chunk)
            row_half(at, 0)
            second_columns(row_thirds, row_second, row_panel)
            row_half(at, 1)
            for k in range(2):
                schur_half(at, k)

        for copy in panel_copies:
            copy.start()
        schur_copy.start()
    for copy in panel_copies:
        copy.wait()
    schur_copy.wait()


def per_device(points, pivots_first, pivots_second):
    per_dev = points.shape[1]
    n_row = lax.axis_size("row")
    n_col = lax.axis_size("col")
    rows_n = per_dev * n_col
    cols_n = per_dev * n_row
    n_piv = pivots_first.shape[0] + pivots_second.shape[0]
    n_tab = n_row * n_col * per_dev * DIM // LANES
    vmem = pl.BlockSpec(memory_space=pltpu.VMEM)
    params = pltpu.CompilerParams(vmem_limit_bytes=VMEM_BYTES)
    copies, *found = pl.pallas_call(
        pack_kernel,
        out_shape=(
            jax.ShapeDtypeStruct((n_tab, LANES), F32),
            jax.ShapeDtypeStruct((n_piv, n_tab), BF16),
            jax.ShapeDtypeStruct((n_piv, LANES), F32),
            jax.ShapeDtypeStruct((SUB, n_piv), jnp.int32),
            jax.ShapeDtypeStruct((3 * LANES, 3 * LANES), BF16),
        ),
        in_specs=[pl.BlockSpec(memory_space=pltpu.HBM)] * 3,
        out_specs=(vmem,) * 5,
        scratch_shapes=[
            pltpu.VMEM((DIM, per_dev), F32),
            pltpu.VMEM((1, pivots_first.shape[0]), jnp.int32),
            pltpu.VMEM((1, pivots_second.shape[0]), jnp.int32),
            pltpu.SemaphoreType.DMA((3,)),
        ],
        compiler_params=params,
        name="pack",
    )(*(pltpu.with_memory_space_constraint(x, pltpu.HBM) for x in (points, pivots_first[None, :], pivots_second[None, :])))
    table = lax.all_to_all(copies, ("row", "col"), 0, 0, tiled=True)
    table, *found = lax.optimization_barrier((table, *found))
    chunk = min(rows_n, 256)
    half = n_piv // 2
    return pl.pallas_call(
        per_device_kernel,
        out_shape=(jax.ShapeDtypeStruct((rows_n, n_piv), F32), jax.ShapeDtypeStruct((rows_n, cols_n), F32)),
        in_specs=[vmem] * 5,
        out_specs=(pl.BlockSpec(memory_space=pl.ANY),) * 2,
        scratch_shapes=[
            [pltpu.VMEM((half, half), F32)] * 2,
            [pltpu.VMEM((half, half), BF16)] * 6,
            pltpu.VMEM((3, half, half), BF16),
            pltpu.VMEM((rows_n, n_piv), F32),
            pltpu.VMEM((rows_n, cols_n), F32),
            pltpu.VMEM((cols_n, LANES), BF16),
            pltpu.VMEM((3, cols_n, n_piv), BF16),
            pltpu.VMEM((3, chunk, n_piv), BF16),
            pltpu.VMEM((cols_n, half), F32),
            pltpu.VMEM((chunk, half), F32),
            pltpu.VMEM((3, cols_n, n_piv), BF16),
            pltpu.VMEM((3, chunk, n_piv), BF16),
            pltpu.SemaphoreType.DMA((3,)),
        ],
        compiler_params=params,
        name="pivoted_cholesky",
    )(table, *found)


def solution(mesh):
    return jax.shard_map(
        per_device,
        mesh=mesh,
        in_specs=(P(None, ("row", "col")), P(), P()),
        out_specs=(P("row", None), P("row", "col")),
        check_vma=False,
    )
```
